512 devices in a mesh: crop: 16 (over x, z_hi, core), seq: 32 (over y, z_lo).
Axes of the slice: x: 4, y: 4, z: 16 (z_hi: 2, z_lo: 8; z = z_hi * 8 + z_lo), core: 2. Of those that a mesh axis runs over, the one named last changes fastest.
Arguments:
- queries: bfloat16 [65536, 2048], P(('crop', 'seq')), parts along dimension 0, may hold values from -13 to 13
- keys: bfloat16 [65536, 2048], P(('crop', 'seq')), parts along dimension 0, may hold values from -6 to 6
- values: bfloat16 [65536, 2048], P(('crop', 'seq')), parts along dimension 0, may hold values from -6 to 6
- proj_weight: bfloat16 [2048, 256], replicated, may hold values from -0.125 to 0.125
- norm_gain: float32 [256], replicated, may hold values from 0.1 to 1.9
- conv_weight: bfloat16 [9, 256, 256], replicated, may hold values from -0.125 to 0.125
- conv_bias: float32 [256], replicated, may hold values from -3 to 3
- class_weight: bfloat16 [9, 16, 256], replicated, may hold values from -4.5 to 4.5
- class_bias: float32 [16], replicated, may hold values from -4 to 4
- labels: int32 [4096, 256], P(('crop', 'seq')), parts along dimension 0, may hold values from 0 to 15
Outputs:
- logits: float32 [16, 4096, 256], P(None, ('crop', 'seq')), parts along dimension 1
- pixel_loss: float32 [4096, 256], P(('crop', 'seq')), parts along dimension 0
- loss: float32 [16], P('crop'), parts along dimension 0
The draws below stay inside these ranges and needn't reach their ends.
There are 16 independent parts, one for each index of `crop`. The reference program is written for one: setup_inputs(seed, part) draws one part's arguments, and reference() takes and returns one part's arrays. A program takes and returns all parts, laid end to end along the dimension named above; an argument that names none is the same for every part. Nothing has to cross between parts.
All inputs are finite; a program needn't handle non-finite values.
Results may differ from the reference program's by a relative error of at most 0.0085.
The reference program's roundings to bfloat16 on the way count: a program that leaves them out, or rounds other values in their place, can miss the bound.
Values may be sent and summed in bfloat16 or wider, within the bound.
No kernel may reach another device: no remote copies, remote signals or barrier semaphores. Data moves between devices by JAX's collectives and lax.ppermute only.
A program may use at most 64 MiB of HBM per device.

```python
import math
import jax
import jax.numpy as jnp
from jax import lax

HEADS = 16
HEAD_DIM = 128
CHANNELS = 256
CLASSES = 16
UPSCALE = 4
GRID_COLS = 64
GRID_ROWS = 64
TOKENS = 4096
PIX_ROWS = 256
PIX_COLS = 256


def paired_draw(key):
    shape = (TOKENS, HEADS * HEAD_DIM)
    key_base = jnp.clip(jax.random.normal(jax.random.fold_in(key, 11), shape, jnp.float32), -6.0, 6.0)
    query_base = jnp.clip(jax.random.normal(jax.random.fold_in(key, 12), shape, jnp.float32), -6.0, 6.0)
    return (query_base, key_base)


def draw_queries(key, part):
    return paired_draw(key)[0].astype(jnp.bfloat16)


def draw_keys(key, part):
    return paired_draw(key)[1].astype(jnp.bfloat16)


def draw_class_weight(key, part):
    shape = (9, CLASSES, CHANNELS)
    spread = 2.0 * CHANNELS ** (-0.5)
    drawn = jnp.clip(jax.random.normal(jax.random.fold_in(key, 34), shape, jnp.float32), -6.0, 6.0) * spread
    return drawn.astype(jnp.bfloat16)


def plant(values, key, smallest, top_value):
    extent = values.shape
    place = [jax.random.randint(jax.random.fold_in(key, axis), (), 0, extent[axis]) for axis in range(len(extent))]
    values = values.at[tuple(place)].set(smallest)
    longest = extent.index(max(extent))
    place[longest] = (place[longest] + 1) % extent[longest]
    return values.at[tuple(place)].set(top_value)


def block_levels(own_key, shape, split, smallest, top_value):
    def one(position, shards_of):
        draws = jax.random.uniform(jax.random.fold_in(jax.random.fold_in(own_key, 6), position), (shards_of,), jnp.float32, smallest / len(split), top_value / len(split))
        return jnp.repeat(jnp.exp(draws), shape[position] // shards_of).reshape((-1,) + (1,) * (len(shape) - position - 1))

    factor_of = one(*split[0])
    for cut in split[1:]:
        factor_of = factor_of * one(*cut)
    return factor_of


def noise(stream_key, extent, width, bound, shards=(), kind=jnp.bfloat16):
    entries = jax.random.normal(stream_key, extent, jnp.float32) * width
    if len(shards) > 0:
        entries = block_levels(stream_key, extent, shards, -0.22, 0.18) * entries
    return jnp.clip(entries, min=-bound, max=bound).astype(kind)


def setup_inputs(seed: int = 0, part: int = 0) -> dict:
    key_of = jax.random.split(jax.random.key(seed), 11)
    part_keys = jax.random.split(jax.random.fold_in(key_of[10], part), 11)
    return {
        "queries": draw_queries(jax.random.fold_in(jax.random.fold_in(key_of[10], part), 71), part),
        "keys": draw_keys(jax.random.fold_in(jax.random.fold_in(key_of[10], part), 71), part),
        "values": noise(part_keys[2], (TOKENS, HEADS * HEAD_DIM), 1.0, 6.0, ((0, 32),)),
        "proj_weight": noise(key_of[3], (HEADS * HEAD_DIM, CHANNELS), (HEADS * HEAD_DIM) ** -0.5, 0.125),
        "norm_gain": jnp.clip(1.0 + 0.18 * jax.random.normal(key_of[4], (CHANNELS,), jnp.float32), 0.1, 1.9),
        "conv_weight": noise(key_of[5], (9, CHANNELS, CHANNELS), (9 * CHANNELS) ** -0.5, 0.125),
        "conv_bias": noise(key_of[6], (CHANNELS,), 0.5, 3.0, (), jnp.float32),
        "class_weight": draw_class_weight(jax.random.fold_in(key_of[10], 71), part),
        "class_bias": noise(key_of[8], (CLASSES,), 1.0, 4.0, (), jnp.float32),
        "labels": plant(jax.random.randint(part_keys[9], (PIX_ROWS, PIX_COLS), 0, CLASSES), jax.random.fold_in(part_keys[9], 1), 0, CLASSES - 1).astype(jnp.int32),
    }


EPSILON = 1e-05

def rotate(packed, row_ids, col_ids):
    count_rows = packed.shape[0]
    head_rows = packed.reshape(count_rows, HEADS, HEAD_DIM).astype(jnp.float32)
    quarter = HEAD_DIM // 4
    omegas = jnp.power(jnp.float32(100.0), -jnp.arange(quarter, dtype=jnp.float32) / quarter)
    pieces = []
    for coords, offset in ((row_ids, 0), (col_ids, 2 * quarter)):
        angles = coords.astype(jnp.float32)[:, None, None] * omegas[None, None, :]
        cosine = jnp.cos(angles)
        sine_part = jnp.sin(angles)
        first_half = head_rows[:, :, offset:offset + quarter]
        second_half = head_rows[:, :, offset + quarter:offset + 2 * quarter]
        pieces.append(first_half * cosine - second_half * sine_part)
        pieces.append(second_half * cosine + first_half * sine_part)
    return jnp.concatenate(pieces, axis=2).reshape(count_rows, HEADS * HEAD_DIM).astype(jnp.bfloat16)

def attend(queries, keys, values):
    total_rows = queries.shape[0]
    block = math.gcd(512, total_rows)
    scale = queries.shape[2] ** (-0.5)
    keys_wide = keys.astype(jnp.float32)
    values_wide = values.astype(jnp.float32)

    def one_block(query_block):
        scores = jnp.einsum('qhd,khd->hqk', query_block.astype(jnp.float32), keys_wide) * scale
        highest = lax.optimization_barrier(jnp.max(scores, axis=2, keepdims=True))
        exponent = jnp.exp(scores - highest)
        weights = (exponent / lax.optimization_barrier(jnp.sum(exponent, axis=2, keepdims=True))).astype(jnp.bfloat16)
        mixed = jnp.einsum('hqk,khd->qhd', weights.astype(jnp.float32), values_wide)
        return mixed.astype(jnp.bfloat16)
    blocked = queries.reshape(total_rows // block, block, queries.shape[1], queries.shape[2])
    return lax.map(one_block, blocked).reshape(queries.shape)

def normalize(features, gain):
    center = lax.optimization_barrier(jnp.mean(features, axis=-1, keepdims=True))
    spread = lax.optimization_barrier(jnp.mean((features - center) ** 2, axis=-1, keepdims=True))
    return (features - center) / jnp.sqrt(spread + EPSILON) * gain

def convolve(padded, weight):
    out_rows = padded.shape[0] - 2
    out_cols = padded.shape[1] - 2
    summed = jnp.zeros((out_rows * out_cols, weight.shape[2]), jnp.float32)
    for tap_index in range(9):
        tap_row, tap_col = (tap_index // 3, tap_index % 3)
        window = padded[tap_row:tap_row + out_rows, tap_col:tap_col + out_cols].reshape(-1, padded.shape[2])
        summed = summed + jnp.dot(window, weight[tap_index], preferred_element_type=jnp.float32)
    return summed.reshape(out_rows, out_cols, weight.shape[2])

def classify(padded, class_weight):
    out_rows = padded.shape[0] - 2
    out_cols = padded.shape[1] - 2
    summed = jnp.zeros((class_weight.shape[1], out_rows * out_cols), jnp.float32)
    for tap_index in range(9):
        tap_row, tap_col = (tap_index // 3, tap_index % 3)
        window = padded[tap_row:tap_row + out_rows, tap_col:tap_col + out_cols].reshape(-1, padded.shape[2])
        summed = summed + lax.dot_general(class_weight[tap_index], window, (((1,), (1,)), ((), ())), preferred_element_type=jnp.float32)
    return summed.reshape(class_weight.shape[1], out_rows, out_cols)

def pixel_losses(logits, labels):
    highest = lax.optimization_barrier(jnp.max(logits, axis=0))
    log_total = highest + jnp.log(lax.optimization_barrier(jnp.sum(jnp.exp(logits - highest[None]), axis=0)))
    class_ids = jnp.arange(logits.shape[0], dtype=jnp.int32)[:, None, None]
    picked = lax.optimization_barrier(jnp.sum(jnp.where(class_ids == labels[None], logits, jnp.zeros_like(logits)), axis=0))
    return log_total - picked

def reference(queries, keys, values, proj_weight, norm_gain, conv_weight, conv_bias, class_weight, class_bias, labels):
    positions = jnp.arange(TOKENS, dtype=jnp.int32)
    row_ids = positions // GRID_COLS
    col_ids = positions % GRID_COLS
    rotated_queries = rotate(queries, row_ids, col_ids).reshape(TOKENS, HEADS, HEAD_DIM)
    rotated_keys = rotate(keys, row_ids, col_ids).reshape(TOKENS, HEADS, HEAD_DIM)
    mixed = attend(rotated_queries, rotated_keys, values.reshape(TOKENS, HEADS, HEAD_DIM))
    mixed = mixed.reshape(TOKENS, HEADS * HEAD_DIM)
    features = jnp.dot(mixed, proj_weight, preferred_element_type=jnp.float32)
    activated = jax.nn.gelu(normalize(features, norm_gain), approximate=False).astype(jnp.bfloat16)
    activated = activated.reshape(GRID_ROWS, GRID_COLS, -1)
    padded = jnp.pad(activated, ((1, 1), (1, 1), (0, 0)))
    hidden = jax.nn.gelu(convolve(padded, conv_weight) + conv_bias, approximate=False).astype(jnp.bfloat16)
    upsampled = jnp.repeat(jnp.repeat(hidden, UPSCALE, axis=0), UPSCALE, axis=1)
    logits = classify(jnp.pad(upsampled, ((1, 1), (1, 1), (0, 0))), class_weight) + class_bias[:, None, None]
    losses = pixel_losses(logits, labels)
    loss = (jnp.sum(losses) / (PIX_ROWS * PIX_COLS)).reshape(1)
    return (logits, losses, loss)
```

```python
import functools
import math

import jax
import jax.numpy as jnp
import numpy as np
from jax import lax
from jax.experimental import pallas as pl
from jax.experimental.pallas import tpu as pltpu
from jax.sharding import Mesh, PartitionSpec as P

HEADS = 16
HEAD_DIM = 128
UPSCALE = 4
COLS = 64
CHANNELS = 256
CLASSES = 16
YS = 4
ZS = 8
SEQ = YS * ZS
EPSILON = 1e-05
EXP_SCALE = HEAD_DIM**-0.5 * math.log2(math.e)
VMEM = pl.BlockSpec(memory_space=pltpu.VMEM)
SMEM = pl.BlockSpec(memory_space=pltpu.SMEM)
BF16 = jnp.bfloat16
F32 = jnp.float32


def rotary_tables():
    quarter = HEAD_DIM // 4
    omegas = np.power(np.float32(100.0), -np.arange(quarter, dtype=np.float32) / np.float32(quarter))
    angles = np.arange(COLS, dtype=np.float32)[:, None] * omegas[None, :].astype(np.float32)
    cosine = np.cos(angles).astype(np.float32)
    sine = np.sin(angles).astype(np.float32)
    wide_cos = np.concatenate([cosine] * 4, axis=1)
    wide_sin = np.concatenate([-sine, sine, -sine, sine], axis=1)
    return wide_cos, wide_sin


def gelu(x):
    return x * (0.5 * (1.0 + lax.erf(x * np.float32(math.sqrt(0.5)))))


def pack_kernel(info, q_ref, k_ref, v_ref, cos_ref, sin_ref, out_ref):
    core = info[0]
    place = info[1]
    lane = lax.broadcasted_iota(jnp.int32, (COLS, HEAD_DIM), 1)
    by_row = lane < HEAD_DIM // 2
    first = (lane % (HEAD_DIM // 2)) < HEAD_DIM // 4
    for half in range(2):
        row_id = 2 * place + half
        cosine = jnp.where(by_row, cos_ref[pl.ds(row_id, 1), :], cos_ref[...])
        sine = jnp.where(by_row, sin_ref[pl.ds(row_id, 1), :], sin_ref[...])
        rows = slice(half * COLS, (half + 1) * COLS)
        for sub in range(2):
            lanes = slice(sub * HEAD_DIM, (sub + 1) * HEAD_DIM)
            y = lax.rem(2 * sub + half + core, YS)
            for index, ref in ((0, q_ref), (1, k_ref)):
                x = ref[rows, lanes].astype(F32)
                partner = jnp.where(
                    first,
                    pltpu.roll(x, HEAD_DIM - HEAD_DIM // 4, 1),
                    pltpu.roll(x, HEAD_DIM // 4, 1),
                )
                out_ref[y, 0, index * COLS : (index + 1) * COLS, :] = (
                    x * cosine + partner * sine
                ).astype(BF16)
            out_ref[y, 0, 2 * COLS :, :] = v_ref[rows, lanes]


def pack(info, queries, keys, values, cosine, sine):
    tokens = queries.shape[0]
    wide = 2 * HEAD_DIM
    return pl.pallas_call(
        pack_kernel,
        grid_spec=pltpu.PrefetchScalarGridSpec(
            num_scalar_prefetch=1,
            grid=(ZS,),
            in_specs=[pl.BlockSpec((tokens, wide), lambda z, info: (0, z))] * 3
            + [pl.BlockSpec((COLS, HEAD_DIM), lambda z, info: (0, 0))] * 2,
            out_specs=pl.BlockSpec((YS, 1, 3 * COLS, HEAD_DIM), lambda z, info: (0, z, 0, 0)),
        ),
        out_shape=jax.ShapeDtypeStruct((YS, ZS, 3 * COLS, HEAD_DIM), BF16),
        name="pack",
    )(info, queries, keys, values, cosine, sine)


BLOCK = 4


def scores_of(query, key):
    return lax.dot_general(query, key, (((1,), (1,)), ((), ())), preferred_element_type=F32)


def with_ones(value):
    return jnp.concatenate([value, jnp.ones_like(value)], axis=1)


def own_kernel(mine_ref, acc_ref, top_ref):
    rows = BLOCK * COLS
    key = mine_ref[:, COLS : 2 * COLS, :].reshape(SEQ * COLS, HEAD_DIM)
    value = with_ones(mine_ref[:, 2 * COLS :, :].reshape(SEQ * COLS, HEAD_DIM))

    def step(i, carry):
        query = mine_ref[pl.ds(i * BLOCK, BLOCK), :COLS, :].reshape(rows, HEAD_DIM)
        scores = scores_of(query, key)
        top = jnp.max(scores, axis=1, keepdims=True)
        weights = jnp.exp2((scores - top) * EXP_SCALE).astype(BF16)
        out = pl.ds(pl.multiple_of(i * rows, rows), rows)
        acc_ref[out, :] = jnp.dot(weights, value, preferred_element_type=F32)
        top_ref[out, :] = jnp.broadcast_to(top, (rows, HEAD_DIM))
        return carry

    lax.fori_loop(0, SEQ // BLOCK, step, 0)


def other_kernel(mine_ref, other_ref, acc_ref, top_ref, out_ref):
    rows = BLOCK * COLS
    key = other_ref[:, :COLS, :].reshape(SEQ * COLS, HEAD_DIM)
    value = with_ones(other_ref[:, COLS:, :].reshape(SEQ * COLS, HEAD_DIM))

    def step(i, carry):
        query = mine_ref[pl.ds(i * BLOCK, BLOCK), :COLS, :].reshape(rows, HEAD_DIM)
        scores = scores_of(query, key)
        place = pl.ds(pl.multiple_of(i * rows, rows), rows)
        before = top_ref[place, :1]
        top = jnp.maximum(before, jnp.max(scores, axis=1, keepdims=True))
        weights = jnp.exp2((scores - top) * EXP_SCALE).astype(BF16)
        fade = jnp.exp2((before - top) * EXP_SCALE)
        total = acc_ref[place, :] * fade + jnp.dot(weights, value, preferred_element_type=F32)
        mixed = total[:, :HEAD_DIM] / total[:, HEAD_DIM:]
        out_ref[pl.ds(i * BLOCK, BLOCK), :, :] = mixed.astype(BF16).reshape(BLOCK, COLS, HEAD_DIM)
        return carry

    lax.fori_loop(0, SEQ // BLOCK, step, 0)


def attend(mine, swap):
    tokens = SEQ * COLS
    half_flops = 2 * tokens * tokens * HEAD_DIM * 3
    cost = pl.CostEstimate(flops=half_flops, bytes_accessed=4 << 20, transcendentals=tokens * tokens)
    other = swap(mine[:, COLS:, :])
    acc, top = pl.pallas_call(
        own_kernel,
        in_specs=[VMEM],
        out_specs=[VMEM, VMEM],
        out_shape=[
            jax.ShapeDtypeStruct((tokens, 2 * HEAD_DIM), F32),
            jax.ShapeDtypeStruct((tokens, HEAD_DIM), F32),
        ],
        cost_estimate=cost,
        name="own_keys",
    )(mine)
    return pl.pallas_call(
        other_kernel,
        in_specs=[VMEM] * 4,
        out_specs=VMEM,
        out_shape=jax.ShapeDtypeStruct((SEQ, COLS, HEAD_DIM), BF16),
        cost_estimate=cost,
        name="other_keys",
    )(mine, other, acc, top)


def features_kernel(info, mixed_ref, proj_ref, gain_ref, out_ref):
    core = info[0]
    strips = []
    for half in range(2):
        pieces = []
        for head in range(HEADS):
            y = lax.rem(2 * (head % 2) + half + core, YS)
            pieces.append(mixed_ref[y * ZS + head // 2])
        strips.append(jnp.concatenate(pieces, axis=1))
    mixed = jnp.concatenate(strips, axis=0)
    features = jnp.dot(mixed, proj_ref[...], preferred_element_type=F32)
    center = jnp.mean(features, axis=-1, keepdims=True)
    spread = jnp.mean((features - center) ** 2, axis=-1, keepdims=True)
    normal = (features - center) / jnp.sqrt(spread + EPSILON) * gain_ref[...]
    out_ref[...] = gelu(normal).astype(BF16)


def head_kernel(
    info, low_ref, mid_ref, high_ref, weight_ref, bias_ref, class_ref, class_bias_ref, labels_ref,
    logits_ref, losses_ref, sum_ref,
):
    place = info[1]
    strip = 2
    act = jnp.concatenate([low_ref[...], mid_ref[...], high_ref[...]], axis=0)
    count = (strip + 2) * COLS
    stacked = jnp.concatenate([act[r * COLS : r * COLS + count] for r in range(3)], axis=1)
    products = []
    for s in range(3):
        weight = jnp.concatenate([weight_ref[3 * r + s] for r in range(3)], axis=0)
        products.append(jnp.dot(stacked, weight, preferred_element_type=F32))
    position = lax.broadcasted_iota(jnp.int32, (count, CHANNELS), 0)
    col = position % COLS
    total = products[1]
    total = total + jnp.where(col == 0, 0.0, pltpu.roll(products[0], 1, 0))
    total = total + jnp.where(col == COLS - 1, 0.0, pltpu.roll(products[2], count - 1, 0))
    hidden = gelu(total + bias_ref[...])
    grid_row = place * strip - 1 + position // COLS
    inside = (grid_row >= 0) & (grid_row < strip * SEQ)
    hidden = jnp.where(inside, hidden, 0.0).astype(BF16)

    taps = lax.dot_general(
        class_ref[...], hidden, (((1,), (1,)), ((), ())), preferred_element_type=F32
    )

    def tap(r, s, row):
        start = (3 * r + s) * CLASSES
        return taps[start : start + CLASSES, row * COLS : (row + 1) * COLS]

    sides = []
    for s in range(3):
        combos = []
        for row in (1, 2):
            t = [tap(r, s, row) for r in range(3)]
            combos.append(tap(0, s, row - 1) + t[1] + t[2])
            combos.append(t[0] + t[1] + t[2])
            combos.append(t[0] + t[1] + tap(2, s, row + 1))
        sides.append(jnp.concatenate(combos, axis=0))
    pixels = UPSCALE * COLS
    source = lax.broadcasted_iota(jnp.int32, (COLS, pixels), 0)
    target = lax.broadcasted_iota(jnp.int32, (COLS, pixels), 1)
    spread_sum = None
    for s, side in enumerate(sides):
        first = UPSCALE * source - s + 1
        expand = jnp.where((target >= first) & (target < first + UPSCALE), 1.0, 0.0).astype(BF16)
        for _ in range(3):
            part = side.astype(BF16)
            side = side - part.astype(F32)
            term = jnp.dot(part, expand, preferred_element_type=F32)
            spread_sum = term if spread_sum is None else spread_sum + term
    class_ids = lax.broadcasted_iota(jnp.int32, (CLASSES, pixels), 0)
    loss_sum = jnp.zeros((1, pixels), F32)
    for y in range(UPSCALE * strip):
        combo = 3 * (y // UPSCALE) + (0, 1, 1, 2)[y % UPSCALE]
        logits = spread_sum[combo * CLASSES : (combo + 1) * CLASSES] + class_bias_ref[...]
        logits_ref[:, y, :] = logits
        highest = jnp.max(logits, axis=0, keepdims=True)
        log_total = highest + jnp.log(jnp.sum(jnp.exp(logits - highest), axis=0, keepdims=True))
        chosen = class_ids == labels_ref[y : y + 1, :]
        picked = jnp.sum(jnp.where(chosen, logits, 0.0), axis=0, keepdims=True)
        loss = log_total - picked
        losses_ref[y : y + 1, :] = loss
        loss_sum = loss_sum + loss
    total_loss = jnp.sum(loss_sum, axis=1, keepdims=True)
    sum_ref[...] = jnp.broadcast_to(total_loss[None], sum_ref.shape)


def body(
    mesh_shape, queries, keys, values, proj_weight, norm_gain, conv_weight, conv_bias, class_weight,
    class_bias, labels,
):
    place = lax.axis_index(("y", "z"))
    core = lax.rem(lax.axis_index("crop"), 2)
    info = jnp.stack([core, place]).astype(jnp.int32)
    cosine, sine = rotary_tables()
    crops = mesh_shape["crop"]
    seq = ("y", "z")

    swaps = []
    for crop in range(crops):
        for y in range(YS):
            slot = (y - crop % 2) % YS
            swaps.append((crop * YS + y, crop * YS + ((slot ^ 1) + crop % 2) % YS))

    send = pack(info, queries, keys, values, cosine, sine).reshape(SEQ, 3 * COLS, HEAD_DIM)
    mine = lax.all_to_all(send, seq, 0, 0, tiled=True)
    attended = attend(mine, lambda x: lax.ppermute(x, ("crop", "y"), swaps))
    returned = lax.all_to_all(attended, seq, 0, 0, tiled=True)

    strip_tokens = queries.shape[0]
    act = pl.pallas_call(
        features_kernel,
        in_specs=[SMEM] + [VMEM] * 3,
        out_specs=VMEM,
        out_shape=jax.ShapeDtypeStruct((strip_tokens, CHANNELS), BF16),
        name="features",
    )(info, returned, proj_weight, norm_gain.reshape(1, CHANNELS))
    low = lax.ppermute(act, seq, [(i, i + 1) for i in range(SEQ - 1)])
    high = lax.ppermute(act, seq, [(i + 1, i) for i in range(SEQ - 1)])
    rows, pixels = labels.shape
    logits, losses, sums = pl.pallas_call(
        head_kernel,
        in_specs=[SMEM] + [VMEM] * 8,
        out_specs=[VMEM] * 3,
        out_shape=[
            jax.ShapeDtypeStruct((CLASSES, rows, pixels), F32),
            jax.ShapeDtypeStruct((rows, pixels), F32),
            jax.ShapeDtypeStruct((SEQ, 1, HEAD_DIM), F32),
        ],
        name="head",
    )(
        info, low, act, high, conv_weight, conv_bias.reshape(1, CHANNELS),
        class_weight.reshape(9 * CLASSES, CHANNELS), class_bias.reshape(CLASSES, 1), labels,
    )
    everyone = lax.all_to_all(sums, seq, 0, 0, tiled=True)
    loss = (jnp.sum(everyone[:, 0, 0]) / (rows * pixels * SEQ)).reshape(1)
    return logits, losses, loss


def solution(mesh):
    crops = mesh.shape["crop"]
    split = Mesh(mesh.devices.reshape(crops, YS, ZS), ("crop", "y", "z"))
    rows = P(("crop", "y", "z"), None)
    in_specs = (rows, rows, rows, P(), P(), P(), P(), P(), P(), rows)
    out_specs = (P(None, ("crop", "y", "z"), None), rows, P("crop"))
    return jax.shard_map(
        functools.partial(body, dict(split.shape)),
        mesh=split,
        in_specs=in_specs,
        out_specs=out_specs,
        check_vma=False,
    )
```

```python
import functools
import math

import jax
import jax.numpy as jnp
import numpy as np
from jax import lax
from jax.experimental import pallas as pl
from jax.experimental.pallas import tpu as pltpu
from jax.sharding import Mesh, PartitionSpec as P


HEADS = 16
HEAD_DIM = 128
UPSCALE = 4
COLS = 64
CHANNELS = 256
CLASSES = 16
YS = 4
ZS = 8
SEQ = YS * ZS
EPSILON = 1e-05
EXP_SCALE = HEAD_DIM**-0.5 * math.log2(math.e)
VMEM = pl.BlockSpec(memory_space=pltpu.VMEM)
BF16 = jnp.bfloat16
F32 = jnp.float32


def limit(mib):
    return pltpu.CompilerParams(vmem_limit_bytes=mib << 20)


def rotary_tables():
    quarter = HEAD_DIM // 4
    omegas = np.power(np.float32(100.0), -np.arange(quarter, dtype=np.float32) / np.float32(quarter))
    angles = np.arange(COLS, dtype=np.float32)[:, None] * omegas[None, :].astype(np.float32)
    cosine = np.cos(angles).astype(np.float32)
    sine = np.sin(angles).astype(np.float32)
    wide_cos = np.concatenate([cosine] * 4, axis=1)
    wide_sin = np.concatenate([-sine, sine, -sine, sine], axis=1)
    return wide_cos, wide_sin


def gelu(x):
    return x * (0.5 * (1.0 + lax.erf(x * np.float32(math.sqrt(0.5)))))


def positions():
    place = lax.axis_index("y") * ZS + lax.axis_index("z")
    return lax.rem(lax.axis_index("crop"), 2), place


def pack_kernel(q_ref, k_ref, v_ref, cos_ref, sin_ref, out_ref):
    core, place = positions()
    lane = lax.broadcasted_iota(jnp.int32, (COLS, HEAD_DIM), 1)
    by_row = lane < HEAD_DIM // 2
    first = (lane % (HEAD_DIM // 2)) < HEAD_DIM // 4
    tables = []
    for half in range(2):
        row = pl.ds(2 * place + half, 1)
        tables.append(
            [jnp.where(by_row, ref[row, :], ref[...]) for ref in (cos_ref, sin_ref)]
        )

    def step(z, carry):
        for sub in range(2):
            lanes = pl.ds(pl.multiple_of((2 * z + sub) * HEAD_DIM, HEAD_DIM), HEAD_DIM)
            for half in range(2):
                cosine, sine = tables[half]
                rows = slice(half * COLS, (half + 1) * COLS)
                y = lax.rem(2 * sub + half + core, YS)
                for index, ref in ((0, q_ref), (1, k_ref)):
                    x = ref[rows, lanes].astype(F32)
                    partner = jnp.where(
                        first,
                        pltpu.roll(x, HEAD_DIM - HEAD_DIM // 4, 1),
                        pltpu.roll(x, HEAD_DIM // 4, 1),
                    )
                    out_ref[y, z, index * COLS : (index + 1) * COLS, :] = (
                        x * cosine + partner * sine
                    ).astype(BF16)
                out_ref[y, z, 2 * COLS :, :] = v_ref[rows, lanes]
        return carry

    lax.fori_loop(0, ZS, step, 0, unroll=2)


def pack(queries, keys, values, cosine, sine):
    return pl.pallas_call(
        pack_kernel,
        in_specs=[VMEM] * 5,
        out_specs=VMEM,
        out_shape=jax.ShapeDtypeStruct((YS, ZS, 3 * COLS, HEAD_DIM), BF16),
        compiler_params=limit(8),
        name="pack",
    )(queries, keys, values, cosine, sine)


BLOCK = 4


def scores_of(query, key):
    return lax.dot_general(query, key, (((1,), (1,)), ((), ())), preferred_element_type=F32)


def with_ones(value):
    return jnp.concatenate([value, jnp.ones_like(value)], axis=1)


CHUNK = 512


def sweep(query, key_ref, value, top, total):
    for start in range(0, SEQ * COLS, CHUNK):
        scores = scores_of(query, key_ref[start : start + CHUNK])
        before, top = top, jnp.max(scores, axis=1, keepdims=True)
        if before is not None:
            top = jnp.maximum(before, top)
        weights = jnp.exp2((scores - top) * EXP_SCALE).astype(BF16)
        part = jnp.dot(weights, value[start : start + CHUNK], preferred_element_type=F32)
        total = part if before is None else total * jnp.exp2((before - top) * EXP_SCALE) + part
    return top, total


def own_kernel(mine_ref, acc_ref, top_ref):
    rows = BLOCK * COLS
    key = mine_ref[:, COLS : 2 * COLS, :].reshape(SEQ * COLS, HEAD_DIM)
    value = with_ones(mine_ref[:, 2 * COLS :, :].reshape(SEQ * COLS, HEAD_DIM))

    def step(i, carry):
        query = mine_ref[pl.ds(i * BLOCK, BLOCK), :COLS, :].reshape(rows, HEAD_DIM)
        top, total = sweep(query, key, value, None, None)
        out = pl.ds(pl.multiple_of(i * rows, rows), rows)
        acc_ref[out, :] = total
        top_ref[out, :] = jnp.broadcast_to(top, (rows, HEAD_DIM))
        return carry

    lax.fori_loop(0, SEQ // BLOCK, step, 0, unroll=4)


def other_kernel(mine_ref, other_ref, acc_ref, top_ref, out_ref):
    rows = BLOCK * COLS
    key = other_ref[:, :COLS, :].reshape(SEQ * COLS, HEAD_DIM)
    value = with_ones(other_ref[:, COLS:, :].reshape(SEQ * COLS, HEAD_DIM))

    def step(i, carry):
        query = mine_ref[pl.ds(i * BLOCK, BLOCK), :COLS, :].reshape(rows, HEAD_DIM)
        place = pl.ds(pl.multiple_of(i * rows, rows), rows)
        _, total = sweep(query, key, value, top_ref[place, :1], acc_ref[place, :])
        mixed = total[:, :HEAD_DIM] / total[:, HEAD_DIM:]
        out_ref[pl.ds(i * BLOCK, BLOCK), :, :] = mixed.astype(BF16).reshape(BLOCK, COLS, HEAD_DIM)
        return carry

    lax.fori_loop(0, SEQ // BLOCK, step, 0, unroll=4)


def attend(mine, swap):
    tokens = SEQ * COLS
    half_flops = 2 * tokens * tokens * HEAD_DIM * 3
    cost = pl.CostEstimate(flops=half_flops, bytes_accessed=4 << 20, transcendentals=tokens * tokens)
    other = swap(mine[:, COLS:, :])
    acc, top = pl.pallas_call(
        own_kernel,
        in_specs=[VMEM],
        out_specs=[VMEM, VMEM],
        out_shape=[
            jax.ShapeDtypeStruct((tokens, 2 * HEAD_DIM), F32),
            jax.ShapeDtypeStruct((tokens, HEAD_DIM), F32),
        ],
        cost_estimate=cost,
        compiler_params=limit(28),
        name="own_keys",
    )(mine)
    return pl.pallas_call(
        other_kernel,
        in_specs=[VMEM] * 4,
        out_specs=VMEM,
        out_shape=jax.ShapeDtypeStruct((SEQ, COLS, HEAD_DIM), BF16),
        cost_estimate=cost,
        compiler_params=limit(28),
        name="other_keys",
    )(mine, other, acc, top)


def features_kernel(mixed_ref, proj_ref, gain_ref, out_ref):
    core, _ = positions()
    strips = []
    for half in range(2):
        pieces = []
        for head in range(HEADS):
            y = lax.rem(2 * (head % 2) + half + core, YS)
            pieces.append(mixed_ref[y * ZS + head // 2])
        strips.append(jnp.concatenate(pieces, axis=1))
    mixed = jnp.concatenate(strips, axis=0)
    features = jnp.dot(mixed, proj_ref[...], preferred_element_type=F32)
    center = jnp.mean(features, axis=-1, keepdims=True)
    spread = jnp.mean((features - center) ** 2, axis=-1, keepdims=True)
    normal = (features - center) / jnp.sqrt(spread + EPSILON) * gain_ref[...]
    out_ref[...] = gelu(normal).astype(BF16)


def head_kernel(
    pair_ref, mid_ref, far_ref, weight_ref, bias_ref, class_ref, class_bias_ref, labels_ref,
    logits_ref, losses_ref, sum_ref, act,
):
    _, place = positions()
    strip = 2
    odd = lax.rem(place, 2)
    edge = 2 * strip * COLS
    act[pl.ds(pl.multiple_of((1 - odd) * edge, strip * COLS), strip * COLS), :] = pair_ref[...]
    act[strip * COLS : edge, :] = mid_ref[...]
    act[pl.ds(pl.multiple_of(odd * edge, strip * COLS), strip * COLS), :] = far_ref[...]
    count = (strip + 2) * COLS
    stacked = jnp.concatenate([act[r * COLS : r * COLS + count] for r in range(3)], axis=1)
    products = []
    for s in range(3):
        weight = jnp.concatenate([weight_ref[3 * r + s] for r in range(3)], axis=0)
        products.append(jnp.dot(stacked, weight, preferred_element_type=F32))
    position = lax.broadcasted_iota(jnp.int32, (count, CHANNELS), 0)
    col = position % COLS
    total = products[1]
    total = total + jnp.where(col == 0, 0.0, pltpu.roll(products[0], 1, 0))
    total = total + jnp.where(col == COLS - 1, 0.0, pltpu.roll(products[2], count - 1, 0))
    hidden = gelu(total + bias_ref[...])
    grid_row = place * strip - 1 + position // COLS
    inside = (grid_row >= 0) & (grid_row < strip * SEQ)
    hidden = jnp.where(inside, hidden, 0.0).astype(BF16)

    taps = lax.dot_general(
        class_ref[...], hidden, (((1,), (1,)), ((), ())), preferred_element_type=F32
    )

    def tap(r, s, row):
        start = (3 * r + s) * CLASSES
        return taps[start : start + CLASSES, row * COLS : (row + 1) * COLS]

    sides = []
    for s in range(3):
        combos = []
        for row in (1, 2):
            t = [tap(r, s, row) for r in range(3)]
            combos.append(tap(0, s, row - 1) + t[1] + t[2])
            combos.append(t[0] + t[1] + t[2])
            combos.append(t[0] + t[1] + tap(2, s, row + 1))
        sides.append(jnp.concatenate(combos, axis=0))
    pixels = UPSCALE * COLS
    source = lax.broadcasted_iota(jnp.int32, (COLS, pixels), 0)
    target = lax.broadcasted_iota(jnp.int32, (COLS, pixels), 1)
    spread_sum = None
    for s, side in enumerate(sides):
        first = UPSCALE * source - s + 1
        expand = jnp.where((target >= first) & (target < first + UPSCALE), 1.0, 0.0).astype(BF16)
        for _ in range(3):
            part = side.astype(BF16)
            side = side - part.astype(F32)
            term = jnp.dot(part, expand, preferred_element_type=F32)
            spread_sum = term if spread_sum is None else spread_sum + term
    class_ids = lax.broadcasted_iota(jnp.int32, (CLASSES, pixels), 0)
    loss_sum = jnp.zeros((1, pixels), F32)
    for y in range(UPSCALE * strip):
        combo = 3 * (y // UPSCALE) + (0, 1, 1, 2)[y % UPSCALE]
        logits = spread_sum[combo * CLASSES : (combo + 1) * CLASSES] + class_bias_ref[...]
        logits_ref[:, y, :] = logits
        highest = jnp.max(logits, axis=0, keepdims=True)
        log_total = highest + jnp.log(jnp.sum(jnp.exp(logits - highest), axis=0, keepdims=True))
        chosen = class_ids == labels_ref[y : y + 1, :]
        picked = jnp.sum(jnp.where(chosen, logits, 0.0), axis=0, keepdims=True)
        loss = log_total - picked
        losses_ref[y : y + 1, :] = loss
        loss_sum = loss_sum + loss
    total_loss = jnp.sum(loss_sum, axis=1, keepdims=True)
    sum_ref[...] = jnp.broadcast_to(total_loss[None], sum_ref.shape)


def body(
    mesh_shape, queries, keys, values, proj_weight, norm_gain, conv_weight, conv_bias, class_weight,
    class_bias, labels,
):
    cosine, sine = rotary_tables()
    crops = mesh_shape["crop"]
    seq = ("y", "z")

    swaps = []
    for crop in range(crops):
        for y in range(YS):
            slot = (y - crop % 2) % YS
            swaps.append((crop * YS + y, crop * YS + ((slot ^ 1) + crop % 2) % YS))

    send = pack(queries, keys, values, cosine, sine).reshape(SEQ, 3 * COLS, HEAD_DIM)
    mine = lax.all_to_all(send, seq, 0, 0, tiled=True)
    attended = attend(mine, lambda x: lax.ppermute(x, ("crop", "y"), swaps))
    returned = lax.all_to_all(attended, seq, 0, 0, tiled=True)

    strip_tokens = queries.shape[0]
    act = pl.pallas_call(
        features_kernel,
        in_specs=[VMEM] * 3,
        out_specs=VMEM,
        out_shape=jax.ShapeDtypeStruct((strip_tokens, CHANNELS), BF16),
        compiler_params=limit(12),
        name="features",
    )(returned, proj_weight, norm_gain.reshape(1, CHANNELS))
    far = lax.ppermute(act, seq, [(i, ((i + 1) ^ 1) - 1) for i in range(1, SEQ - 1)])
    pair = lax.ppermute(act, seq, [(i, i ^ 1) for i in range(SEQ)])
    rows, pixels = labels.shape
    logits, losses, sums = pl.pallas_call(
        head_kernel,
        in_specs=[VMEM] * 8,
        out_specs=[VMEM] * 3,
        out_shape=[
            jax.ShapeDtypeStruct((CLASSES, rows, pixels), F32),
            jax.ShapeDtypeStruct((rows, pixels), F32),
            jax.ShapeDtypeStruct((SEQ, 1, HEAD_DIM), F32),
        ],
        scratch_shapes=[pltpu.VMEM((3 * strip_tokens, CHANNELS), BF16)],
        compiler_params=limit(12),
        name="head",
    )(
        pair, act, far, conv_weight, conv_bias.reshape(1, CHANNELS),
        class_weight.reshape(9 * CLASSES, CHANNELS), class_bias.reshape(CLASSES, 1), labels,
    )
    everyone = lax.all_to_all(sums, seq, 0, 0, tiled=True)
    loss = (jnp.sum(everyone[:, 0, 0]) / (rows * pixels * SEQ)).reshape(1)
    return logits, losses, loss


def solution(mesh):
    crops = mesh.shape["crop"]
    split = Mesh(mesh.devices.reshape(crops, YS, ZS), ("crop", "y", "z"))
    rows = P(("crop", "y", "z"), None)
    in_specs = (rows, rows, rows, P(), P(), P(), P(), P(), P(), rows)
    out_specs = (P(None, ("crop", "y", "z"), None), rows, P("crop"))
    return jax.shard_map(
        functools.partial(body, dict(split.shape)),
        mesh=split,
        in_specs=in_specs,
        out_specs=out_specs,
        check_vma=False,
    )
```

```python
import functools
import math

import jax
import jax.numpy as jnp
import numpy as np
from jax import lax
from jax.experimental import pallas as pl
from jax.experimental.pallas import tpu as pltpu
from jax.sharding import Mesh, PartitionSpec as P


HEADS = 16
HEAD_DIM = 128
UPSCALE = 4
COLS = 64
CHANNELS = 256
CLASSES = 16
YS = 4
ZS = 8
SEQ = YS * ZS
EPSILON = 1e-05
EXP_SCALE = HEAD_DIM**-0.5 * math.log2(math.e)
VMEM = pl.BlockSpec(memory_space=pltpu.VMEM)
BF16 = jnp.bfloat16
F32 = jnp.float32


def limit(mib):
    return pltpu.CompilerParams(vmem_limit_bytes=mib << 20)


def rotary_tables():
    quarter = HEAD_DIM // 4
    omegas = np.power(np.float32(100.0), -np.arange(quarter, dtype=np.float32) / np.float32(quarter))
    angles = np.arange(COLS, dtype=np.float32)[:, None] * omegas[None, :].astype(np.float32)
    cosine = np.cos(angles).astype(np.float32)
    sine = np.sin(angles).astype(np.float32)
    wide_cos = np.concatenate([cosine] * 4, axis=1)
    wide_sin = np.concatenate([-sine, sine, -sine, sine], axis=1)
    return wide_cos, wide_sin


def gelu(x):
    return x * (0.5 * (1.0 + lax.erf(x * np.float32(math.sqrt(0.5)))))


def positions():
    place = lax.axis_index("y") * ZS + lax.axis_index("z")
    return lax.rem(lax.axis_index("crop"), 2), place


PARTS = 4
PART = HEADS * HEAD_DIM // PARTS


def pack_kernel(q_hbm, k_hbm, v_hbm, cos_hbm, sin_hbm, out_ref, q_ref, k_ref, v_ref, cos_ref, sin_ref, sems, table_sems):
    core, place = positions()
    tables_in = [
        pltpu.make_async_copy(cos_hbm, cos_ref, table_sems.at[0]),
        pltpu.make_async_copy(sin_hbm, sin_ref, table_sems.at[1]),
    ]
    for copy in tables_in:
        copy.start()
    copies = []
    for part in range(PARTS):
        lanes = pl.ds(part * PART, PART)
        copies.append(
            [
                pltpu.make_async_copy(hbm.at[:, lanes], ref.at[part], sems.at[part, which])
                for which, (hbm, ref) in enumerate(((q_hbm, q_ref), (k_hbm, k_ref), (v_hbm, v_ref)))
            ]
        )
        for copy in copies[-1]:
            copy.start()
    lane = lax.broadcasted_iota(jnp.int32, (COLS, HEAD_DIM), 1)
    by_row = lane < HEAD_DIM // 2
    first = (lane % (HEAD_DIM // 2)) < HEAD_DIM // 4
    for copy in tables_in:
        copy.wait()
    tables = []
    for half in range(2):
        row = pl.ds(2 * place + half, 1)
        tables.append(
            [jnp.where(by_row, ref[row, :], ref[...]) for ref in (cos_ref, sin_ref)]
        )
    for part in range(PARTS):
        for copy in copies[part]:
            copy.wait()
        for inner in range(HEADS // PARTS):
            head = part * (HEADS // PARTS) + inner
            z = head // 2
            lanes = slice(inner * HEAD_DIM, (inner + 1) * HEAD_DIM)
            for half in range(2):
                cosine, sine = tables[half]
                rows = slice(half * COLS, (half + 1) * COLS)
                y = lax.rem(2 * (head % 2) + half + core, YS)
                for index, ref in ((0, q_ref), (1, k_ref)):
                    x = ref[part, rows, lanes].astype(F32)
                    partner = jnp.where(
                        first,
                        pltpu.roll(x, HEAD_DIM - HEAD_DIM // 4, 1),
                        pltpu.roll(x, HEAD_DIM // 4, 1),
                    )
                    out_ref[y, z, index * COLS : (index + 1) * COLS, :] = (
                        x * cosine + partner * sine
                    ).astype(BF16)
                out_ref[y, z, 2 * COLS :, :] = v_ref[part, rows, lanes]


def pack(queries, keys, values, cosine, sine):
    tokens = queries.shape[0]
    return pl.pallas_call(
        pack_kernel,
        in_specs=[pl.BlockSpec(memory_space=pltpu.HBM)] * 5,
        out_specs=VMEM,
        out_shape=jax.ShapeDtypeStruct((YS, ZS, 3 * COLS, HEAD_DIM), BF16),
        scratch_shapes=[pltpu.VMEM((PARTS, tokens, PART), BF16)] * 3
        + [pltpu.VMEM((COLS, HEAD_DIM), F32)] * 2
        + [pltpu.SemaphoreType.DMA((PARTS, 3)), pltpu.SemaphoreType.DMA((2,))],
        compiler_params=limit(8),
        name="pack",
    )(*(pltpu.with_memory_space_constraint(x, pltpu.HBM) for x in (queries, keys, values, cosine, sine)))


BLOCK = 4


def scores_of(query, key):
    return lax.dot_general(query, key, (((1,), (1,)), ((), ())), preferred_element_type=F32)


def with_ones(value):
    return jnp.concatenate([value, jnp.ones_like(value)], axis=1)


CHUNK = 512


def sweep(query, key, value):
    top = total = None
    for start in range(0, key.shape[0], CHUNK):
        scores = scores_of(query, key[start : start + CHUNK])
        before, top = top, jnp.max(scores, axis=1, keepdims=True)
        if before is not None:
            top = jnp.maximum(before, top)
        weights = jnp.exp2((scores - top) * EXP_SCALE).astype(BF16)
        part = jnp.dot(weights, value[start : start + CHUNK], preferred_element_type=F32)
        total = part if before is None else total * jnp.exp2((before - top) * EXP_SCALE) + part
    return jnp.broadcast_to(top, (query.shape[0], HEAD_DIM)), total


def own_kernel(mine_ref, acc_ref, top_ref):
    rows = BLOCK * COLS
    key = mine_ref[:, COLS : 2 * COLS, :].reshape(SEQ * COLS, HEAD_DIM)
    value = with_ones(mine_ref[:, 2 * COLS :, :].reshape(SEQ * COLS, HEAD_DIM))

    def step(i, carry):
        query = mine_ref[pl.ds(i * BLOCK, BLOCK), :COLS, :].reshape(rows, HEAD_DIM)
        out = pl.ds(pl.multiple_of(i * rows, rows), rows)
        top_ref[out, :], acc_ref[out, :] = sweep(query, key, value)
        return carry

    lax.fori_loop(0, SEQ // BLOCK, step, 0, unroll=SEQ // BLOCK)


def other_kernel(mine_ref, other_ref, acc_ref, top_ref, out_ref):
    rows = BLOCK * COLS
    key = other_ref[:, :COLS, :].reshape(SEQ * COLS, HEAD_DIM)
    value = with_ones(other_ref[:, COLS:, :].reshape(SEQ * COLS, HEAD_DIM))

    def step(i, carry):
        query = mine_ref[pl.ds(i * BLOCK, BLOCK), :COLS, :].reshape(rows, HEAD_DIM)
        place = pl.ds(pl.multiple_of(i * rows, rows), rows)
        top_here, here = sweep(query, key, value)
        top_there, there = top_ref[place, :], acc_ref[place, :]
        top = jnp.maximum(top_here, top_there)
        fade_here = jnp.exp2((top_here - top) * EXP_SCALE)
        fade_there = jnp.exp2((top_there - top) * EXP_SCALE)
        mixed = here[:, :HEAD_DIM] * fade_here + there[:, :HEAD_DIM] * fade_there
        norm = here[:, HEAD_DIM:] * fade_here + there[:, HEAD_DIM:] * fade_there
        out_ref[pl.ds(i * BLOCK, BLOCK), :, :] = (
            (mixed / norm).astype(BF16).reshape(BLOCK, COLS, HEAD_DIM)
        )
        return carry

    lax.fori_loop(0, SEQ // BLOCK, step, 0, unroll=SEQ // BLOCK)


def attend(mine, swap):
    tokens = SEQ * COLS
    half_flops = 2 * tokens * tokens * HEAD_DIM * 3
    cost = pl.CostEstimate(flops=half_flops, bytes_accessed=4 << 20, transcendentals=tokens * tokens)
    other = swap(mine[:, COLS:, :])
    acc, top = pl.pallas_call(
        own_kernel,
        in_specs=[VMEM],
        out_specs=[VMEM, VMEM],
        out_shape=[
            jax.ShapeDtypeStruct((tokens, 2 * HEAD_DIM), F32),
            jax.ShapeDtypeStruct((tokens, HEAD_DIM), F32),
        ],
        cost_estimate=cost,
        compiler_params=limit(28),
        name="own_keys",
    )(mine)
    return pl.pallas_call(
        other_kernel,
        in_specs=[VMEM] * 4,
        out_specs=VMEM,
        out_shape=jax.ShapeDtypeStruct((SEQ, COLS, HEAD_DIM), BF16),
        cost_estimate=cost,
        compiler_params=limit(28),
        name="other_keys",
    )(mine, other, acc, top)


def features_kernel(mixed_ref, proj_ref, gain_ref, out_ref):
    core, _ = positions()
    strips = []
    for half in range(2):
        pieces = []
        for head in range(HEADS):
            y = lax.rem(2 * (head % 2) + half + core, YS)
            pieces.append(mixed_ref[y * ZS + head // 2])
        strips.append(jnp.concatenate(pieces, axis=1))
    mixed = jnp.concatenate(strips, axis=0)
    features = jnp.dot(mixed, proj_ref[...], preferred_element_type=F32)
    center = jnp.mean(features, axis=-1, keepdims=True)
    spread = jnp.mean((features - center) ** 2, axis=-1, keepdims=True)
    normal = (features - center) / jnp.sqrt(spread + EPSILON) * gain_ref[...]
    out_ref[...] = gelu(normal).astype(BF16)


def head_kernel(
    pair_ref, mid_ref, far_ref, weight_ref, bias_ref, class_ref, class_bias_ref, labels_ref,
    logits_ref, losses_ref, sum_ref, act,
):
    _, place = positions()
    strip = 2
    odd = lax.rem(place, 2)
    edge = 2 * strip * COLS
    act[pl.ds(pl.multiple_of((1 - odd) * edge, strip * COLS), strip * COLS), :] = pair_ref[...]
    act[strip * COLS : edge, :] = mid_ref[...]
    act[pl.ds(pl.multiple_of(odd * edge, strip * COLS), strip * COLS), :] = far_ref[...]
    count = (strip + 2) * COLS
    stacked = jnp.concatenate([act[r * COLS : r * COLS + count] for r in range(3)], axis=1)
    products = []
    for s in range(3):
        weight = jnp.concatenate([weight_ref[3 * r + s] for r in range(3)], axis=0)
        products.append(jnp.dot(stacked, weight, preferred_element_type=F32))
    position = lax.broadcasted_iota(jnp.int32, (count, CHANNELS), 0)
    col = position % COLS
    total = products[1]
    total = total + jnp.where(col == 0, 0.0, pltpu.roll(products[0], 1, 0))
    total = total + jnp.where(col == COLS - 1, 0.0, pltpu.roll(products[2], count - 1, 0))
    hidden = gelu(total + bias_ref[...])
    grid_row = place * strip - 1 + position // COLS
    inside = (grid_row >= 0) & (grid_row < strip * SEQ)
    hidden = jnp.where(inside, hidden, 0.0).astype(BF16)

    taps = lax.dot_general(
        class_ref[...], hidden, (((1,), (1,)), ((), ())), preferred_element_type=F32
    )

    def tap(r, s, row):
        start = (3 * r + s) * CLASSES
        return taps[start : start + CLASSES, row * COLS : (row + 1) * COLS]

    sides = []
    for s in range(3):
        combos = []
        for row in (1, 2):
            t = [tap(r, s, row) for r in range(3)]
            combos.append(tap(0, s, row - 1) + t[1] + t[2])
            combos.append(t[0] + t[1] + t[2])
            combos.append(t[0] + t[1] + tap(2, s, row + 1))
        sides.append(jnp.concatenate(combos, axis=0))
    pixels = UPSCALE * COLS
    source = lax.broadcasted_iota(jnp.int32, (COLS, pixels), 0)
    target = lax.broadcasted_iota(jnp.int32, (COLS, pixels), 1)
    spread_sum = None
    for s, side in enumerate(sides):
        first = UPSCALE * source - s + 1
        expand = jnp.where((target >= first) & (target < first + UPSCALE), 1.0, 0.0).astype(BF16)
        for _ in range(3):
            part = side.astype(BF16)
            side = side - part.astype(F32)
            term = jnp.dot(part, expand, preferred_element_type=F32)
            spread_sum = term if spread_sum is None else spread_sum + term
    class_ids = lax.broadcasted_iota(jnp.int32, (CLASSES, pixels), 0)
    loss_sum = jnp.zeros((1, pixels), F32)
    for y in range(UPSCALE * strip):
        combo = 3 * (y // UPSCALE) + (0, 1, 1, 2)[y % UPSCALE]
        logits = spread_sum[combo * CLASSES : (combo + 1) * CLASSES] + class_bias_ref[...]
        logits_ref[:, y, :] = logits
        highest = jnp.max(logits, axis=0, keepdims=True)
        log_total = highest + jnp.log(jnp.sum(jnp.exp(logits - highest), axis=0, keepdims=True))
        chosen = class_ids == labels_ref[y : y + 1, :]
        picked = jnp.sum(jnp.where(chosen, logits, 0.0), axis=0, keepdims=True)
        loss = log_total - picked
        losses_ref[y : y + 1, :] = loss
        loss_sum = loss_sum + loss
    total_loss = jnp.sum(loss_sum, axis=1, keepdims=True)
    sum_ref[...] = jnp.broadcast_to(total_loss[None], sum_ref.shape)


def body(
    mesh_shape, queries, keys, values, proj_weight, norm_gain, conv_weight, conv_bias, class_weight,
    class_bias, labels,
):
    cosine, sine = rotary_tables()
    crops = mesh_shape["crop"]
    seq = ("y", "z")

    swaps = []
    for crop in range(crops):
        for y in range(YS):
            slot = (y - crop % 2) % YS
            swaps.append((crop * YS + y, crop * YS + ((slot ^ 1) + crop % 2) % YS))

    send = pack(queries, keys, values, cosine, sine).reshape(SEQ, 3 * COLS, HEAD_DIM)
    mine = lax.all_to_all(send, seq, 0, 0, tiled=True)
    attended = attend(mine, lambda x: lax.ppermute(x, ("crop", "y"), swaps))
    returned = lax.all_to_all(attended, seq, 0, 0, tiled=True)

    strip_tokens = queries.shape[0]
    act = pl.pallas_call(
        features_kernel,
        in_specs=[VMEM] * 3,
        out_specs=VMEM,
        out_shape=jax.ShapeDtypeStruct((strip_tokens, CHANNELS), BF16),
        compiler_params=limit(12),
        name="features",
    )(returned, proj_weight, norm_gain.reshape(1, CHANNELS))
    far = lax.ppermute(act, seq, [(i, ((i + 1) ^ 1) - 1) for i in range(1, SEQ - 1)])
    pair = lax.ppermute(act, seq, [(i, i ^ 1) for i in range(SEQ)])
    rows, pixels = labels.shape
    logits, losses, sums = pl.pallas_call(
        head_kernel,
        in_specs=[VMEM] * 8,
        out_specs=[VMEM] * 3,
        out_shape=[
            jax.ShapeDtypeStruct((CLASSES, rows, pixels), F32),
            jax.ShapeDtypeStruct((rows, pixels), F32),
            jax.ShapeDtypeStruct((SEQ, 1, HEAD_DIM), F32),
        ],
        scratch_shapes=[pltpu.VMEM((3 * strip_tokens, CHANNELS), BF16)],
        compiler_params=limit(12),
        name="head",
    )(
        pair, act, far, conv_weight, conv_bias.reshape(1, CHANNELS),
        class_weight.reshape(9 * CLASSES, CHANNELS), class_bias.reshape(CLASSES, 1), labels,
    )
    everyone = lax.all_to_all(sums, seq, 0, 0, tiled=True)
    loss = (jnp.sum(everyone[:, 0, 0]) / (rows * pixels * SEQ)).reshape(1)
    return logits, losses, loss


def solution(mesh):
    crops = mesh.shape["crop"]
    split = Mesh(mesh.devices.reshape(crops, YS, ZS), ("crop", "y", "z"))
    rows = P(("crop", "y", "z"), None)
    in_specs = (rows, rows, rows, P(), P(), P(), P(), P(), P(), rows)
    out_specs = (P(None, ("crop", "y", "z"), None), rows, P("crop"))
    return jax.shard_map(
        functools.partial(body, dict(split.shape)),
        mesh=split,
        in_specs=in_specs,
        out_specs=out_specs,
        check_vma=False,
    )
```

```python
import functools
import math

import jax
import jax.numpy as jnp
import numpy as np
from jax import lax
from jax.experimental import pallas as pl
from jax.experimental.pallas import tpu as pltpu
from jax.sharding import Mesh, PartitionSpec as P


HEADS = 16
HEAD_DIM = 128
UPSCALE = 4
COLS = 64
CHANNELS = 256
CLASSES = 16
YS = 4
ZS = 8
SEQ = YS * ZS
EPSILON = 1e-05
EXP_SCALE = HEAD_DIM**-0.5 * math.log2(math.e)
VMEM = pl.BlockSpec(memory_space=pltpu.VMEM)
BF16 = jnp.bfloat16
F32 = jnp.float32


def limit(mib):
    return pltpu.CompilerParams(vmem_limit_bytes=mib << 20)


def rotary_tables():
    quarter = HEAD_DIM // 4
    omegas = np.power(np.float32(100.0), -np.arange(quarter, dtype=np.float32) / np.float32(quarter))
    angles = np.arange(COLS, dtype=np.float32)[:, None] * omegas[None, :].astype(np.float32)
    cosine = np.cos(angles).astype(np.float32)
    sine = np.sin(angles).astype(np.float32)
    wide_cos = np.concatenate([cosine] * 4, axis=1)
    wide_sin = np.concatenate([-sine, sine, -sine, sine], axis=1)
    return wide_cos, wide_sin


def gelu(x):
    return x * (0.5 * (1.0 + lax.erf(x * np.float32(math.sqrt(0.5)))))


def positions():
    place = lax.axis_index("y") * ZS + lax.axis_index("z")
    return lax.rem(lax.axis_index("crop"), 2), place


LATE = 16
EARLY = COLS - LATE
PARTS = 4
PART = HEADS * HEAD_DIM // PARTS


def pack_kernel(q_hbm, k_hbm, v_hbm, cos_hbm, sin_hbm, out_ref, late_ref, q_ref, k_ref, v_ref, cos_ref, sin_ref, sems, table_sems):
    core, place = positions()
    tables_in = [
        pltpu.make_async_copy(cos_hbm, cos_ref, table_sems.at[0]),
        pltpu.make_async_copy(sin_hbm, sin_ref, table_sems.at[1]),
    ]
    for copy in tables_in:
        copy.start()
    copies = []
    for part in range(PARTS):
        lanes = pl.ds(part * PART, PART)
        copies.append(
            [
                pltpu.make_async_copy(hbm.at[:, lanes], ref.at[part], sems.at[part, which])
                for which, (hbm, ref) in enumerate(((q_hbm, q_ref), (k_hbm, k_ref), (v_hbm, v_ref)))
            ]
        )
        for copy in copies[-1]:
            copy.start()
    lane = lax.broadcasted_iota(jnp.int32, (COLS, HEAD_DIM), 1)
    by_row = lane < HEAD_DIM // 2
    first = (lane % (HEAD_DIM // 2)) < HEAD_DIM // 4
    for copy in tables_in:
        copy.wait()
    tables = []
    for half in range(2):
        row = pl.ds(2 * place + half, 1)
        tables.append(
            [jnp.where(by_row, ref[row, :], ref[...]) for ref in (cos_ref, sin_ref)]
        )
    for part in range(PARTS):
        for copy in copies[part]:
            copy.wait()
        for inner in range(HEADS // PARTS):
            head = part * (HEADS // PARTS) + inner
            z = head // 2
            lanes = slice(inner * HEAD_DIM, (inner + 1) * HEAD_DIM)
            for half in range(2):
                cosine, sine = tables[half]
                rows = slice(half * COLS, (half + 1) * COLS)
                y = lax.rem(2 * (head % 2) + half + core, YS)
                for index, ref in ((0, q_ref), (1, k_ref)):
                    x = ref[part, rows, lanes].astype(F32)
                    partner = jnp.where(
                        first,
                        pltpu.roll(x, HEAD_DIM - HEAD_DIM // 4, 1),
                        pltpu.roll(x, HEAD_DIM // 4, 1),
                    )
                    turned = (x * cosine + partner * sine).astype(BF16)
                    if index == 0:
                        out_ref[y, z, :EARLY, :] = turned[:EARLY]
                        late_ref[y, z, :, :] = turned[EARLY:]
                    else:
                        out_ref[y, z, EARLY : EARLY + COLS, :] = turned
                out_ref[y, z, EARLY + COLS :, :] = v_ref[part, rows, lanes]


def pack(queries, keys, values, cosine, sine):
    tokens = queries.shape[0]
    return pl.pallas_call(
        pack_kernel,
        in_specs=[pl.BlockSpec(memory_space=pltpu.HBM)] * 5,
        out_specs=[VMEM, VMEM],
        out_shape=[
            jax.ShapeDtypeStruct((YS, ZS, EARLY + 2 * COLS, HEAD_DIM), BF16),
            jax.ShapeDtypeStruct((YS, ZS, LATE, HEAD_DIM), BF16),
        ],
        scratch_shapes=[pltpu.VMEM((PARTS, tokens, PART), BF16)] * 3
        + [pltpu.VMEM((COLS, HEAD_DIM), F32)] * 2
        + [pltpu.SemaphoreType.DMA((PARTS, 3)), pltpu.SemaphoreType.DMA((2,))],
        compiler_params=limit(8),
        name="pack",
    )(*(pltpu.with_memory_space_constraint(x, pltpu.HBM) for x in (queries, keys, values, cosine, sine)))


BLOCK = 4


def scores_of(query, key):
    return lax.dot_general(query, key, (((1,), (1,)), ((), ())), preferred_element_type=F32)


def with_ones(value):
    return jnp.concatenate([value, jnp.ones_like(value)], axis=1)


CHUNK = 512


def sweep(query, key, value):
    top = total = None
    for start in range(0, key.shape[0], CHUNK):
        scores = scores_of(query, key[start : start + CHUNK])
        before, top = top, jnp.max(scores, axis=1, keepdims=True)
        if before is not None:
            top = jnp.maximum(before, top)
        weights = jnp.exp2((scores - top) * EXP_SCALE).astype(BF16)
        part = jnp.dot(weights, value[start : start + CHUNK], preferred_element_type=F32)
        total = part if before is None else total * jnp.exp2((before - top) * EXP_SCALE) + part
    return jnp.broadcast_to(top, (query.shape[0], HEAD_DIM)), total


def keys_values(ref, first):
    tokens = SEQ * COLS
    key = ref[:, first : first + COLS, :].reshape(tokens, HEAD_DIM)
    value = ref[:, first + COLS : first + 2 * COLS, :].reshape(tokens, HEAD_DIM)
    return key, with_ones(value)


def joined(one, two):
    top = jnp.maximum(one[0], two[0])
    fades = [jnp.exp2((side[0] - top) * EXP_SCALE) for side in (one, two)]
    mixed, norm = [
        sum(side[1][:, lanes] * fade for side, fade in zip((one, two), fades))
        for lanes in (slice(0, HEAD_DIM), slice(HEAD_DIM, 2 * HEAD_DIM))
    ]
    return (mixed / norm).astype(BF16)


def own_kernel(mine_ref, acc_ref, top_ref):
    rows = BLOCK * EARLY
    key, value = keys_values(mine_ref, EARLY)

    def step(i, carry):
        query = mine_ref[pl.ds(i * BLOCK, BLOCK), :EARLY, :].reshape(rows, HEAD_DIM)
        out = pl.ds(pl.multiple_of(i * rows, rows), rows)
        top_ref[out, :], acc_ref[out, :] = sweep(query, key, value)
        return carry

    lax.fori_loop(0, SEQ // BLOCK, step, 0, unroll=SEQ // BLOCK)


def other_kernel(mine_ref, other_ref, acc_ref, top_ref, out_ref):
    rows = BLOCK * EARLY
    key, value = keys_values(other_ref, 0)

    def step(i, carry):
        query = mine_ref[pl.ds(i * BLOCK, BLOCK), :EARLY, :].reshape(rows, HEAD_DIM)
        place = pl.ds(pl.multiple_of(i * rows, rows), rows)
        mixed = joined(sweep(query, key, value), (top_ref[place, :], acc_ref[place, :]))
        out_ref[pl.ds(i * BLOCK, BLOCK), :EARLY, :] = mixed.reshape(BLOCK, EARLY, HEAD_DIM)
        return carry

    lax.fori_loop(0, SEQ // BLOCK, step, 0, unroll=SEQ // BLOCK)


LATE_BLOCK = 8


def late_kernel(late_ref, mine_ref, other_ref, early_ref, out_ref):
    rows = LATE_BLOCK * LATE
    own = keys_values(mine_ref, EARLY)
    other = keys_values(other_ref, 0)
    del early_ref
    for i in range(SEQ // LATE_BLOCK):
        block = slice(i * LATE_BLOCK, (i + 1) * LATE_BLOCK)
        query = late_ref[block].reshape(rows, HEAD_DIM)
        mixed = joined(sweep(query, *own), sweep(query, *other))
        out_ref[block, EARLY:, :] = mixed.reshape(LATE_BLOCK, LATE, HEAD_DIM)


def attend(send, late, swap, everyone):
    tokens = SEQ * EARLY
    cost = pl.CostEstimate(
        flops=6 * tokens * SEQ * COLS * HEAD_DIM,
        bytes_accessed=4 << 20,
        transcendentals=tokens * SEQ * COLS,
    )
    mine = everyone(send)
    other = swap(mine[:, EARLY:, :])
    late = everyone(late)
    acc, top = pl.pallas_call(
        own_kernel,
        in_specs=[VMEM],
        out_specs=[VMEM, VMEM],
        out_shape=[
            jax.ShapeDtypeStruct((tokens, 2 * HEAD_DIM), F32),
            jax.ShapeDtypeStruct((tokens, HEAD_DIM), F32),
        ],
        cost_estimate=cost,
        compiler_params=limit(28),
        name="own_keys",
    )(mine)
    early = pl.pallas_call(
        other_kernel,
        in_specs=[VMEM] * 4,
        out_specs=VMEM,
        out_shape=jax.ShapeDtypeStruct((SEQ, COLS, HEAD_DIM), BF16),
        cost_estimate=cost,
        compiler_params=limit(28),
        name="other_keys",
    )(mine, other, acc, top)
    return pl.pallas_call(
        late_kernel,
        in_specs=[VMEM] * 4,
        out_specs=VMEM,
        out_shape=jax.ShapeDtypeStruct((SEQ, COLS, HEAD_DIM), BF16),
        input_output_aliases={3: 0},
        compiler_params=limit(28),
        name="late_queries",
    )(late, mine, other, early)


def features_kernel(mixed_ref, proj_ref, gain_ref, out_ref):
    core, _ = positions()
    strips = []
    for half in range(2):
        pieces = []
        for head in range(HEADS):
            y = lax.rem(2 * (head % 2) + half + core, YS)
            pieces.append(mixed_ref[y * ZS + head // 2])
        strips.append(jnp.concatenate(pieces, axis=1))
    mixed = jnp.concatenate(strips, axis=0)
    features = jnp.dot(mixed, proj_ref[...], preferred_element_type=F32)
    center = jnp.mean(features, axis=-1, keepdims=True)
    spread = jnp.mean((features - center) ** 2, axis=-1, keepdims=True)
    normal = (features - center) / jnp.sqrt(spread + EPSILON) * gain_ref[...]
    out_ref[...] = gelu(normal).astype(BF16)


def head_kernel(
    pair_ref, mid_ref, far_ref, weight_ref, bias_ref, class_ref, class_bias_ref, labels_ref,
    logits_ref, losses_ref, sum_ref, act,
):
    _, place = positions()
    strip = 2
    odd = lax.rem(place, 2)
    edge = 2 * strip * COLS
    act[pl.ds(pl.multiple_of((1 - odd) * edge, strip * COLS), strip * COLS), :] = pair_ref[...]
    act[strip * COLS : edge, :] = mid_ref[...]
    act[pl.ds(pl.multiple_of(odd * edge, strip * COLS), strip * COLS), :] = far_ref[...]
    count = (strip + 2) * COLS
    stacked = jnp.concatenate([act[r * COLS : r * COLS + count] for r in range(3)], axis=1)
    products = []
    for s in range(3):
        weight = jnp.concatenate([weight_ref[3 * r + s] for r in range(3)], axis=0)
        products.append(jnp.dot(stacked, weight, preferred_element_type=F32))
    position = lax.broadcasted_iota(jnp.int32, (count, CHANNELS), 0)
    col = position % COLS
    total = products[1]
    total = total + jnp.where(col == 0, 0.0, pltpu.roll(products[0], 1, 0))
    total = total + jnp.where(col == COLS - 1, 0.0, pltpu.roll(products[2], count - 1, 0))
    hidden = gelu(total + bias_ref[...])
    grid_row = place * strip - 1 + position // COLS
    inside = (grid_row >= 0) & (grid_row < strip * SEQ)
    hidden = jnp.where(inside, hidden, 0.0).astype(BF16)

    taps = lax.dot_general(
        class_ref[...], hidden, (((1,), (1,)), ((), ())), preferred_element_type=F32
    )

    def tap(r, s, row):
        start = (3 * r + s) * CLASSES
        return taps[start : start + CLASSES, row * COLS : (row + 1) * COLS]

    sides = []
    for s in range(3):
        combos = []
        for row in (1, 2):
            t = [tap(r, s, row) for r in range(3)]
            combos.append(tap(0, s, row - 1) + t[1] + t[2])
            combos.append(t[0] + t[1] + t[2])
            combos.append(t[0] + t[1] + tap(2, s, row + 1))
        sides.append(jnp.concatenate(combos, axis=0))
    pixels = UPSCALE * COLS
    source = lax.broadcasted_iota(jnp.int32, (COLS, pixels), 0)
    target = lax.broadcasted_iota(jnp.int32, (COLS, pixels), 1)
    spread_sum = None
    for s, side in enumerate(sides):
        first = UPSCALE * source - s + 1
        expand = jnp.where((target >= first) & (target < first + UPSCALE), 1.0, 0.0).astype(BF16)
        for _ in range(3):
            part = side.astype(BF16)
            side = side - part.astype(F32)
            term = jnp.dot(part, expand, preferred_element_type=F32)
            spread_sum = term if spread_sum is None else spread_sum + term
    class_ids = lax.broadcasted_iota(jnp.int32, (CLASSES, pixels), 0)
    loss_sum = jnp.zeros((1, pixels), F32)
    for y in range(UPSCALE * strip):
        combo = 3 * (y // UPSCALE) + (0, 1, 1, 2)[y % UPSCALE]
        logits = spread_sum[combo * CLASSES : (combo + 1) * CLASSES] + class_bias_ref[...]
        logits_ref[:, y, :] = logits
        highest = jnp.max(logits, axis=0, keepdims=True)
        log_total = highest + jnp.log(jnp.sum(jnp.exp(logits - highest), axis=0, keepdims=True))
        chosen = class_ids == labels_ref[y : y + 1, :]
        picked = jnp.sum(jnp.where(chosen, logits, 0.0), axis=0, keepdims=True)
        loss = log_total - picked
        losses_ref[y : y + 1, :] = loss
        loss_sum = loss_sum + loss
    total_loss = jnp.sum(loss_sum, axis=1, keepdims=True)
    sum_ref[...] = jnp.broadcast_to(total_loss[None], sum_ref.shape)


def body(
    mesh_shape, queries, keys, values, proj_weight, norm_gain, conv_weight, conv_bias, class_weight,
    class_bias, labels,
):
    cosine, sine = rotary_tables()
    crops = mesh_shape["crop"]
    seq = ("y", "z")

    swaps = []
    for crop in range(crops):
        for y in range(YS):
            slot = (y - crop % 2) % YS
            swaps.append((crop * YS + y, crop * YS + ((slot ^ 1) + crop % 2) % YS))

    send, late = (
        x.reshape(SEQ, x.shape[2], HEAD_DIM) for x in pack(queries, keys, values, cosine, sine)
    )
    attended = attend(
        send,
        late,
        lambda x: lax.ppermute(x, ("crop", "y"), swaps),
        lambda x: lax.all_to_all(x, seq, 0, 0, tiled=True),
    )
    returned = lax.all_to_all(attended, seq, 0, 0, tiled=True)

    strip_tokens = queries.shape[0]
    act = pl.pallas_call(
        features_kernel,
        in_specs=[VMEM] * 3,
        out_specs=VMEM,
        out_shape=jax.ShapeDtypeStruct((strip_tokens, CHANNELS), BF16),
        compiler_params=limit(12),
        name="features",
    )(returned, proj_weight, norm_gain.reshape(1, CHANNELS))
    far = lax.ppermute(act, seq, [(i, ((i + 1) ^ 1) - 1) for i in range(1, SEQ - 1)])
    pair = lax.ppermute(act, seq, [(i, i ^ 1) for i in range(SEQ)])
    rows, pixels = labels.shape
    logits, losses, sums = pl.pallas_call(
        head_kernel,
        in_specs=[VMEM] * 8,
        out_specs=[VMEM] * 3,
        out_shape=[
            jax.ShapeDtypeStruct((CLASSES, rows, pixels), F32),
            jax.ShapeDtypeStruct((rows, pixels), F32),
            jax.ShapeDtypeStruct((SEQ, 1, HEAD_DIM), F32),
        ],
        scratch_shapes=[pltpu.VMEM((3 * strip_tokens, CHANNELS), BF16)],
        compiler_params=limit(12),
        name="head",
    )(
        pair, act, far, conv_weight, conv_bias.reshape(1, CHANNELS),
        class_weight.reshape(9 * CLASSES, CHANNELS), class_bias.reshape(CLASSES, 1), labels,
    )
    everyone = lax.all_to_all(sums, seq, 0, 0, tiled=True)
    loss = (jnp.sum(everyone[:, 0, 0]) / (rows * pixels * SEQ)).reshape(1)
    return logits, losses, loss


def solution(mesh):
    crops = mesh.shape["crop"]
    split = Mesh(mesh.devices.reshape(crops, YS, ZS), ("crop", "y", "z"))
    rows = P(("crop", "y", "z"), None)
    in_specs = (rows, rows, rows, P(), P(), P(), P(), P(), P(), rows)
    out_specs = (P(None, ("crop", "y", "z"), None), rows, P("crop"))
    return jax.shard_map(
        functools.partial(body, dict(split.shape)),
        mesh=split,
        in_specs=in_specs,
        out_specs=out_specs,
        check_vma=False,
    )
```

```python
import functools
import math

import jax
import jax.numpy as jnp
import numpy as np
from jax import lax
from jax.experimental import pallas as pl
from jax.experimental.pallas import tpu as pltpu
from jax.sharding import Mesh, PartitionSpec as P


HEADS = 16
HEAD_DIM = 128
UPSCALE = 4
COLS = 64
CHANNELS = 256
CLASSES = 16
YS = 4
ZS = 8
SEQ = YS * ZS
EPSILON = 1e-05
EXP_SCALE = HEAD_DIM**-0.5 * math.log2(math.e)
VMEM = pl.BlockSpec(memory_space=pltpu.VMEM)
BF16 = jnp.bfloat16
F32 = jnp.float32


def limit(mib):
    return pltpu.CompilerParams(vmem_limit_bytes=mib << 20)


def rotary_tables():
    quarter = HEAD_DIM // 4
    omegas = np.power(np.float32(100.0), -np.arange(quarter, dtype=np.float32) / np.float32(quarter))
    angles = np.arange(COLS, dtype=np.float32)[:, None] * omegas[None, :].astype(np.float32)
    cosine = np.cos(angles).astype(np.float32)
    sine = np.sin(angles).astype(np.float32)
    wide_cos = np.concatenate([cosine] * 4, axis=1)
    wide_sin = np.concatenate([-sine, sine, -sine, sine], axis=1)
    return wide_cos, wide_sin


def gelu(x):
    return x * (0.5 * (1.0 + lax.erf(x * np.float32(math.sqrt(0.5)))))


def positions():
    place = lax.axis_index("y") * ZS + lax.axis_index("z")
    return lax.rem(lax.axis_index("crop"), 2), place


PARTS = 4
PART = HEADS * HEAD_DIM // PARTS


def pack_kernel(q_hbm, k_hbm, v_hbm, cos_hbm, sin_hbm, out_ref, q_ref, k_ref, v_ref, cos_ref, sin_ref, sems, table_sems):
    core, place = positions()
    tables_in = [
        pltpu.make_async_copy(cos_hbm, cos_ref, table_sems.at[0]),
        pltpu.make_async_copy(sin_hbm, sin_ref, table_sems.at[1]),
    ]
    for copy in tables_in:
        copy.start()
    copies = []
    for part in range(PARTS):
        lanes = pl.ds(part * PART, PART)
        copies.append(
            [
                pltpu.make_async_copy(hbm.at[:, lanes], ref.at[part], sems.at[part, which])
                for which, (hbm, ref) in enumerate(((q_hbm, q_ref), (k_hbm, k_ref), (v_hbm, v_ref)))
            ]
        )
        for copy in copies[-1]:
            copy.start()
    lane = lax.broadcasted_iota(jnp.int32, (COLS, HEAD_DIM), 1)
    by_row = lane < HEAD_DIM // 2
    first = (lane % (HEAD_DIM // 2)) < HEAD_DIM // 4
    for copy in tables_in:
        copy.wait()
    tables = []
    for half in range(2):
        row = pl.ds(2 * place + half, 1)
        tables.append(
            [jnp.where(by_row, ref[row, :], ref[...]) for ref in (cos_ref, sin_ref)]
        )
    for part in range(PARTS):
        for copy in copies[part]:
            copy.wait()
        for inner in range(HEADS // PARTS):
            head = part * (HEADS // PARTS) + inner
            z = head // 2
            lanes = slice(inner * HEAD_DIM, (inner + 1) * HEAD_DIM)
            for half in range(2):
                cosine, sine = tables[half]
                rows = slice(half * COLS, (half + 1) * COLS)
                y = lax.rem(2 * (head % 2) + half + core, YS)
                for index, ref in ((0, q_ref), (1, k_ref)):
                    x = ref[part, rows, lanes].astype(F32)
                    partner = jnp.where(
                        first,
                        pltpu.roll(x, HEAD_DIM - HEAD_DIM // 4, 1),
                        pltpu.roll(x, HEAD_DIM // 4, 1),
                    )
                    out_ref[y, z, index * COLS : (index + 1) * COLS, :] = (
                        x * cosine + partner * sine
                    ).astype(BF16)
                out_ref[y, z, 2 * COLS :, :] = v_ref[part, rows, lanes]


def pack(queries, keys, values, cosine, sine):
    tokens = queries.shape[0]
    return pl.pallas_call(
        pack_kernel,
        in_specs=[pl.BlockSpec(memory_space=pltpu.HBM)] * 5,
        out_specs=VMEM,
        out_shape=jax.ShapeDtypeStruct((YS, ZS, 3 * COLS, HEAD_DIM), BF16),
        scratch_shapes=[pltpu.VMEM((PARTS, tokens, PART), BF16)] * 3
        + [pltpu.VMEM((COLS, HEAD_DIM), F32)] * 2
        + [pltpu.SemaphoreType.DMA((PARTS, 3)), pltpu.SemaphoreType.DMA((2,))],
        compiler_params=limit(8),
        name="pack",
    )(*(pltpu.with_memory_space_constraint(x, pltpu.HBM) for x in (queries, keys, values, cosine, sine)))


BLOCK = 4


def scores_of(query, key):
    return lax.dot_general(query, key, (((1,), (1,)), ((), ())), preferred_element_type=F32)


def with_ones(value):
    return jnp.concatenate([value, jnp.ones_like(value)], axis=1)


CHUNK = 512


def sweep(query, key, value):
    top = total = None
    for start in range(0, key.shape[0], CHUNK):
        scores = scores_of(query, key[start : start + CHUNK])
        before, top = top, jnp.max(scores, axis=1, keepdims=True)
        if before is not None:
            top = jnp.maximum(before, top)
        weights = jnp.exp2((scores - top) * EXP_SCALE).astype(BF16)
        part = jnp.dot(weights, value[start : start + CHUNK], preferred_element_type=F32)
        total = part if before is None else total * jnp.exp2((before - top) * EXP_SCALE) + part
    return jnp.broadcast_to(top, (query.shape[0], HEAD_DIM)), total


def keys_values(ref, first):
    tokens = ref.shape[0] * COLS
    key = ref[:, first : first + COLS, :].reshape(tokens, HEAD_DIM)
    value = ref[:, first + COLS : first + 2 * COLS, :].reshape(tokens, HEAD_DIM)
    return key, with_ones(value)


def each_block(visit):
    def step(i, carry):
        rows = BLOCK * COLS
        visit(pl.ds(i * BLOCK, BLOCK), pl.ds(pl.multiple_of(i * rows, rows), rows))
        return carry

    lax.fori_loop(0, SEQ // BLOCK, step, 0, unroll=SEQ // BLOCK)


def joined(one, two):
    top = jnp.maximum(one[0], two[0])
    fades = [jnp.exp2((side[0] - top) * EXP_SCALE) for side in (one, two)]
    mixed, norm = [
        one[1][:, lanes] * fades[0] + two[1][:, lanes] * fades[1]
        for lanes in (slice(0, HEAD_DIM), slice(HEAD_DIM, 2 * HEAD_DIM))
    ]
    return top, mixed, norm


def own_kernel(mine_ref, acc_ref, top_ref):
    key, value = keys_values(mine_ref, COLS)

    def visit(block, rows):
        query = mine_ref[block, :COLS, :].reshape(BLOCK * COLS, HEAD_DIM)
        top_ref[rows, :], acc_ref[rows, :] = sweep(query, key, value)

    each_block(visit)


def more_kernel(mine_ref, other_ref, acc_ref, top_ref, new_acc_ref, new_top_ref):
    key, value = keys_values(other_ref, 0)

    def visit(block, rows):
        query = mine_ref[block, :COLS, :].reshape(BLOCK * COLS, HEAD_DIM)
        top, mixed, norm = joined(sweep(query, key, value), (top_ref[rows, :], acc_ref[rows, :]))
        new_top_ref[rows, :] = top
        new_acc_ref[rows, :HEAD_DIM] = mixed
        new_acc_ref[rows, HEAD_DIM:] = norm

    each_block(visit)


def last_kernel(mine_ref, other_ref, acc_ref, top_ref, out_ref):
    key, value = keys_values(other_ref, 0)

    def visit(block, rows):
        query = mine_ref[block, :COLS, :].reshape(BLOCK * COLS, HEAD_DIM)
        _, mixed, norm = joined(sweep(query, key, value), (top_ref[rows, :], acc_ref[rows, :]))
        out_ref[block, :, :] = (mixed / norm).astype(BF16).reshape(BLOCK, COLS, HEAD_DIM)

    each_block(visit)


FIRST = 16


def attend(mine, swap):
    tokens = SEQ * COLS

    def cost(sources):
        pairs = tokens * sources * COLS
        return pl.CostEstimate(flops=6 * pairs * HEAD_DIM, bytes_accessed=4 << 20, transcendentals=pairs)

    running = [
        jax.ShapeDtypeStruct((tokens, 2 * HEAD_DIM), F32),
        jax.ShapeDtypeStruct((tokens, HEAD_DIM), F32),
    ]
    one = swap(mine[:FIRST, COLS:, :])
    two = swap(mine[FIRST:, COLS:, :])
    acc, top = pl.pallas_call(
        own_kernel,
        in_specs=[VMEM],
        out_specs=[VMEM, VMEM],
        out_shape=running,
        cost_estimate=cost(SEQ),
        compiler_params=limit(28),
        name="own_keys",
    )(mine)
    acc, top = pl.pallas_call(
        more_kernel,
        in_specs=[VMEM] * 4,
        out_specs=[VMEM, VMEM],
        out_shape=running,
        cost_estimate=cost(FIRST),
        compiler_params=limit(28),
        name="more_keys",
    )(mine, one, acc, top)
    return pl.pallas_call(
        last_kernel,
        in_specs=[VMEM] * 4,
        out_specs=VMEM,
        out_shape=jax.ShapeDtypeStruct((SEQ, COLS, HEAD_DIM), BF16),
        cost_estimate=cost(SEQ - FIRST),
        compiler_params=limit(28),
        name="last_keys",
    )(mine, two, acc, top)


def features_kernel(mixed_ref, proj_ref, gain_ref, out_ref):
    core, _ = positions()
    strips = []
    for half in range(2):
        pieces = []
        for head in range(HEADS):
            y = lax.rem(2 * (head % 2) + half + core, YS)
            pieces.append(mixed_ref[y * ZS + head // 2])
        strips.append(jnp.concatenate(pieces, axis=1))
    mixed = jnp.concatenate(strips, axis=0)
    features = jnp.dot(mixed, proj_ref[...], preferred_element_type=F32)
    center = jnp.mean(features, axis=-1, keepdims=True)
    spread = jnp.mean((features - center) ** 2, axis=-1, keepdims=True)
    normal = (features - center) / jnp.sqrt(spread + EPSILON) * gain_ref[...]
    out_ref[...] = gelu(normal).astype(BF16)


def head_kernel(
    pair_ref, mid_ref, far_ref, weight_ref, bias_ref, class_ref, class_bias_ref, labels_ref,
    logits_ref, losses_ref, sum_ref, act,
):
    _, place = positions()
    strip = 2
    odd = lax.rem(place, 2)
    edge = 2 * strip * COLS
    act[pl.ds(pl.multiple_of((1 - odd) * edge, strip * COLS), strip * COLS), :] = pair_ref[...]
    act[strip * COLS : edge, :] = mid_ref[...]
    act[pl.ds(pl.multiple_of(odd * edge, strip * COLS), strip * COLS), :] = far_ref[...]
    count = (strip + 2) * COLS
    stacked = jnp.concatenate([act[r * COLS : r * COLS + count] for r in range(3)], axis=1)
    products = []
    for s in range(3):
        weight = jnp.concatenate([weight_ref[3 * r + s] for r in range(3)], axis=0)
        products.append(jnp.dot(stacked, weight, preferred_element_type=F32))
    position = lax.broadcasted_iota(jnp.int32, (count, CHANNELS), 0)
    col = position % COLS
    total = products[1]
    total = total + jnp.where(col == 0, 0.0, pltpu.roll(products[0], 1, 0))
    total = total + jnp.where(col == COLS - 1, 0.0, pltpu.roll(products[2], count - 1, 0))
    hidden = gelu(total + bias_ref[...])
    grid_row = place * strip - 1 + position // COLS
    inside = (grid_row >= 0) & (grid_row < strip * SEQ)
    hidden = jnp.where(inside, hidden, 0.0).astype(BF16)

    taps = lax.dot_general(
        class_ref[...], hidden, (((1,), (1,)), ((), ())), preferred_element_type=F32
    )

    def tap(r, s, row):
        start = (3 * r + s) * CLASSES
        return taps[start : start + CLASSES, row * COLS : (row + 1) * COLS]

    sides = []
    for s in range(3):
        combos = []
        for row in (1, 2):
            t = [tap(r, s, row) for r in range(3)]
            combos.append(tap(0, s, row - 1) + t[1] + t[2])
            combos.append(t[0] + t[1] + t[2])
            combos.append(t[0] + t[1] + tap(2, s, row + 1))
        sides.append(jnp.concatenate(combos, axis=0))
    pixels = UPSCALE * COLS
    source = lax.broadcasted_iota(jnp.int32, (COLS, pixels), 0)
    target = lax.broadcasted_iota(jnp.int32, (COLS, pixels), 1)
    spread_sum = None
    for s, side in enumerate(sides):
        first = UPSCALE * source - s + 1
        expand = jnp.where((target >= first) & (target < first + UPSCALE), 1.0, 0.0).astype(BF16)
        for _ in range(3):
            part = side.astype(BF16)
            side = side - part.astype(F32)
            term = jnp.dot(part, expand, preferred_element_type=F32)
            spread_sum = term if spread_sum is None else spread_sum + term
    class_ids = lax.broadcasted_iota(jnp.int32, (CLASSES, pixels), 0)
    loss_sum = jnp.zeros((1, pixels), F32)
    for y in range(UPSCALE * strip):
        combo = 3 * (y // UPSCALE) + (0, 1, 1, 2)[y % UPSCALE]
        logits = spread_sum[combo * CLASSES : (combo + 1) * CLASSES] + class_bias_ref[...]
        logits_ref[:, y, :] = logits
        highest = jnp.max(logits, axis=0, keepdims=True)
        log_total = highest + jnp.log(jnp.sum(jnp.exp(logits - highest), axis=0, keepdims=True))
        chosen = class_ids == labels_ref[y : y + 1, :]
        picked = jnp.sum(jnp.where(chosen, logits, 0.0), axis=0, keepdims=True)
        loss = log_total - picked
        losses_ref[y : y + 1, :] = loss
        loss_sum = loss_sum + loss
    total_loss = jnp.sum(loss_sum, axis=1, keepdims=True)
    sum_ref[...] = jnp.broadcast_to(total_loss[None], sum_ref.shape)


def body(
    mesh_shape, queries, keys, values, proj_weight, norm_gain, conv_weight, conv_bias, class_weight,
    class_bias, labels,
):
    cosine, sine = rotary_tables()
    crops = mesh_shape["crop"]
    seq = ("y", "z")

    swaps = []
    for crop in range(crops):
        for y in range(YS):
            slot = (y - crop % 2) % YS
            swaps.append((crop * YS + y, crop * YS + ((slot ^ 1) + crop % 2) % YS))

    send = pack(queries, keys, values, cosine, sine).reshape(SEQ, 3 * COLS, HEAD_DIM)
    mine = lax.all_to_all(send, seq, 0, 0, tiled=True)
    attended = attend(mine, lambda x: lax.ppermute(x, ("crop", "y"), swaps))
    returned = lax.all_to_all(attended, seq, 0, 0, tiled=True)

    strip_tokens = queries.shape[0]
    act = pl.pallas_call(
        features_kernel,
        in_specs=[VMEM] * 3,
        out_specs=VMEM,
        out_shape=jax.ShapeDtypeStruct((strip_tokens, CHANNELS), BF16),
        compiler_params=limit(12),
        name="features",
    )(returned, proj_weight, norm_gain.reshape(1, CHANNELS))
    far = lax.ppermute(act, seq, [(i, ((i + 1) ^ 1) - 1) for i in range(1, SEQ - 1)])
    pair = lax.ppermute(act, seq, [(i, i ^ 1) for i in range(SEQ)])
    rows, pixels = labels.shape
    logits, losses, sums = pl.pallas_call(
        head_kernel,
        in_specs=[VMEM] * 8,
        out_specs=[VMEM] * 3,
        out_shape=[
            jax.ShapeDtypeStruct((CLASSES, rows, pixels), F32),
            jax.ShapeDtypeStruct((rows, pixels), F32),
            jax.ShapeDtypeStruct((SEQ, 1, HEAD_DIM), F32),
        ],
        scratch_shapes=[pltpu.VMEM((3 * strip_tokens, CHANNELS), BF16)],
        compiler_params=limit(12),
        name="head",
    )(
        pair, act, far, conv_weight, conv_bias.reshape(1, CHANNELS),
        class_weight.reshape(9 * CLASSES, CHANNELS), class_bias.reshape(CLASSES, 1), labels,
    )
    everyone = lax.all_to_all(sums, seq, 0, 0, tiled=True)
    loss = (jnp.sum(everyone[:, 0, 0]) / (rows * pixels * SEQ)).reshape(1)
    return logits, losses, loss


def solution(mesh):
    crops = mesh.shape["crop"]
    split = Mesh(mesh.devices.reshape(crops, YS, ZS), ("crop", "y", "z"))
    rows = P(("crop", "y", "z"), None)
    in_specs = (rows, rows, rows, P(), P(), P(), P(), P(), P(), rows)
    out_specs = (P(None, ("crop", "y", "z"), None), rows, P("crop"))
    return jax.shard_map(
        functools.partial(body, dict(split.shape)),
        mesh=split,
        in_specs=in_specs,
        out_specs=out_specs,
        check_vma=False,
    )
```

```python
import functools
import math

import jax
import jax.numpy as jnp
import numpy as np
from jax import lax
from jax.experimental import pallas as pl
from jax.experimental.pallas import tpu as pltpu
from jax.sharding import Mesh, PartitionSpec as P


HEADS = 16
HEAD_DIM = 128
UPSCALE = 4
COLS = 64
CHANNELS = 256
CLASSES = 16
YS = 4
ZS = 8
SEQ = YS * ZS
EPSILON = 1e-05
EXP_SCALE = HEAD_DIM**-0.5 * math.log2(math.e)
VMEM = pl.BlockSpec(memory_space=pltpu.VMEM)
BF16 = jnp.bfloat16
F32 = jnp.float32


def limit(mib):
    return pltpu.CompilerParams(vmem_limit_bytes=mib << 20)


def rotary_tables():
    quarter = HEAD_DIM // 4
    omegas = np.power(np.float32(100.0), -np.arange(quarter, dtype=np.float32) / np.float32(quarter))
    angles = np.arange(COLS, dtype=np.float32)[:, None] * omegas[None, :].astype(np.float32)
    cosine = np.cos(angles).astype(np.float32)
    sine = np.sin(angles).astype(np.float32)
    wide_cos = np.concatenate([cosine] * 4, axis=1)
    wide_sin = np.concatenate([-sine, sine, -sine, sine], axis=1)
    return wide_cos, wide_sin


def gelu(x):
    return x * (0.5 * (1.0 + lax.erf(x * np.float32(math.sqrt(0.5)))))


def positions():
    place = lax.axis_index("y") * ZS + lax.axis_index("z")
    return lax.rem(lax.axis_index("crop"), 2), place


HALVES = 2


def pack_kernel(q_hbm, k_hbm, v_hbm, cos_hbm, sin_hbm, out_ref, q_ref, k_ref, v_ref, cos_ref, sin_ref, sems, table_sems):
    core, place = positions()
    tables_in = [
        pltpu.make_async_copy(cos_hbm, cos_ref, table_sems.at[0]),
        pltpu.make_async_copy(sin_hbm, sin_ref, table_sems.at[1]),
    ]
    copies = []
    for half in range(HALVES):
        rows = pl.ds(half * COLS, COLS)
        copies.append(
            [
                pltpu.make_async_copy(hbm.at[rows], ref.at[rows], sems.at[half, which])
                for which, (hbm, ref) in enumerate(((q_hbm, q_ref), (k_hbm, k_ref), (v_hbm, v_ref)))
            ]
        )
        for copy in copies[-1]:
            copy.start()
        if half == 0:
            for copy in tables_in:
                copy.start()
    lane = lax.broadcasted_iota(jnp.int32, (COLS, HEAD_DIM), 1)
    by_row = lane < HEAD_DIM // 2
    first = (lane % (HEAD_DIM // 2)) < HEAD_DIM // 4
    for copy in tables_in:
        copy.wait()
    for half in range(HALVES):
        row = pl.ds(2 * place + half, 1)
        cosine, sine = [
            jnp.where(by_row, ref[row, :], ref[...]) for ref in (cos_ref, sin_ref)
        ]
        rows = slice(half * COLS, (half + 1) * COLS)
        for index, ref in ((0, q_ref), (1, k_ref), (2, v_ref)):
            copies[half][index].wait()
            for head in range(HEADS):
                y = lax.rem(2 * (head % 2) + half + core, YS)
                x = ref[rows, head * HEAD_DIM : (head + 1) * HEAD_DIM]
                if index < 2:
                    x = x.astype(F32)
                    partner = jnp.where(
                        first,
                        pltpu.roll(x, HEAD_DIM - HEAD_DIM // 4, 1),
                        pltpu.roll(x, HEAD_DIM // 4, 1),
                    )
                    x = (x * cosine + partner * sine).astype(BF16)
                out_ref[y, head // 2, index * COLS : (index + 1) * COLS, :] = x


def pack(queries, keys, values, cosine, sine):
    return pl.pallas_call(
        pack_kernel,
        in_specs=[pl.BlockSpec(memory_space=pltpu.HBM)] * 5,
        out_specs=VMEM,
        out_shape=jax.ShapeDtypeStruct((YS, ZS, 3 * COLS, HEAD_DIM), BF16),
        scratch_shapes=[pltpu.VMEM(queries.shape, BF16)] * 3
        + [pltpu.VMEM((COLS, HEAD_DIM), F32)] * 2
        + [pltpu.SemaphoreType.DMA((HALVES, 3)), pltpu.SemaphoreType.DMA((2,))],
        compiler_params=limit(8),
        name="pack",
    )(*(pltpu.with_memory_space_constraint(x, pltpu.HBM) for x in (queries, keys, values, cosine, sine)))


BLOCK = 4


def scores_of(query, key):
    return lax.dot_general(query, key, (((1,), (1,)), ((), ())), preferred_element_type=F32)


def with_ones(value):
    return jnp.concatenate([value, jnp.ones_like(value)], axis=1)


CHUNK = 512


def sweep(query, key, value):
    top = total = None
    for start in range(0, key.shape[0], CHUNK):
        scores = scores_of(query, key[start : start + CHUNK])
        before, top = top, jnp.max(scores, axis=1, keepdims=True)
        if before is not None:
            top = jnp.maximum(before, top)
        weights = jnp.exp2((scores - top) * EXP_SCALE).astype(BF16)
        part = jnp.dot(weights, value[start : start + CHUNK], preferred_element_type=F32)
        total = part if before is None else total * jnp.exp2((before - top) * EXP_SCALE) + part
    return jnp.broadcast_to(top, (query.shape[0], HEAD_DIM)), total


def keys_values(ref, first):
    tokens = ref.shape[0] * COLS
    key = ref[:, first : first + COLS, :].reshape(tokens, HEAD_DIM)
    value = ref[:, first + COLS : first + 2 * COLS, :].reshape(tokens, HEAD_DIM)
    return key, with_ones(value)


def each_block(visit):
    def step(i, carry):
        rows = BLOCK * COLS
        visit(pl.ds(i * BLOCK, BLOCK), pl.ds(pl.multiple_of(i * rows, rows), rows))
        return carry

    lax.fori_loop(0, SEQ // BLOCK, step, 0, unroll=SEQ // BLOCK)


def joined(one, two):
    top = jnp.maximum(one[0], two[0])
    fades = [jnp.exp2((side[0] - top) * EXP_SCALE) for side in (one, two)]
    mixed, norm = [
        one[1][:, lanes] * fades[0] + two[1][:, lanes] * fades[1]
        for lanes in (slice(0, HEAD_DIM), slice(HEAD_DIM, 2 * HEAD_DIM))
    ]
    return top, mixed, norm


def own_kernel(mine_ref, acc_ref, top_ref):
    key, value = keys_values(mine_ref, COLS)

    def visit(block, rows):
        query = mine_ref[block, :COLS, :].reshape(BLOCK * COLS, HEAD_DIM)
        top_ref[rows, :], acc_ref[rows, :] = sweep(query, key, value)

    each_block(visit)


def more_kernel(mine_ref, other_ref, acc_ref, top_ref, new_acc_ref, new_top_ref):
    key, value = keys_values(other_ref, 0)

    def visit(block, rows):
        query = mine_ref[block, :COLS, :].reshape(BLOCK * COLS, HEAD_DIM)
        top, mixed, norm = joined(sweep(query, key, value), (top_ref[rows, :], acc_ref[rows, :]))
        new_top_ref[rows, :] = top
        new_acc_ref[rows, :HEAD_DIM] = mixed
        new_acc_ref[rows, HEAD_DIM:] = norm

    each_block(visit)


def last_kernel(mine_ref, other_ref, acc_ref, top_ref, out_ref):
    key, value = keys_values(other_ref, 0)

    def visit(block, rows):
        query = mine_ref[block, :COLS, :].reshape(BLOCK * COLS, HEAD_DIM)
        _, mixed, norm = joined(sweep(query, key, value), (top_ref[rows, :], acc_ref[rows, :]))
        out_ref[block, :, :] = (mixed / norm).astype(BF16).reshape(BLOCK, COLS, HEAD_DIM)

    each_block(visit)


FIRST = 20


def attend(mine, swap):
    tokens = SEQ * COLS

    def cost(sources):
        pairs = tokens * sources * COLS
        return pl.CostEstimate(flops=6 * pairs * HEAD_DIM, bytes_accessed=4 << 20, transcendentals=pairs)

    running = [
        jax.ShapeDtypeStruct((tokens, 2 * HEAD_DIM), F32),
        jax.ShapeDtypeStruct((tokens, HEAD_DIM), F32),
    ]
    one = swap(mine[:FIRST, COLS:, :])
    two = swap(mine[FIRST:, COLS:, :])
    acc, top = pl.pallas_call(
        own_kernel,
        in_specs=[VMEM],
        out_specs=[VMEM, VMEM],
        out_shape=running,
        cost_estimate=cost(SEQ),
        compiler_params=limit(28),
        name="own_keys",
    )(mine)
    acc, top = pl.pallas_call(
        more_kernel,
        in_specs=[VMEM] * 4,
        out_specs=[VMEM, VMEM],
        out_shape=running,
        cost_estimate=cost(FIRST),
        compiler_params=limit(28),
        name="more_keys",
    )(mine, one, acc, top)
    return pl.pallas_call(
        last_kernel,
        in_specs=[VMEM] * 4,
        out_specs=VMEM,
        out_shape=jax.ShapeDtypeStruct((SEQ, COLS, HEAD_DIM), BF16),
        cost_estimate=cost(SEQ - FIRST),
        compiler_params=limit(28),
        name="last_keys",
    )(mine, two, acc, top)


def features_kernel(mixed_ref, proj_ref, gain_ref, out_ref):
    core, _ = positions()
    strips = []
    for half in range(2):
        pieces = []
        for head in range(HEADS):
            y = lax.rem(2 * (head % 2) + half + core, YS)
            pieces.append(mixed_ref[y * ZS + head // 2])
        strips.append(jnp.concatenate(pieces, axis=1))
    mixed = jnp.concatenate(strips, axis=0)
    features = jnp.dot(mixed, proj_ref[...], preferred_element_type=F32)
    center = jnp.mean(features, axis=-1, keepdims=True)
    spread = jnp.mean((features - center) ** 2, axis=-1, keepdims=True)
    normal = (features - center) / jnp.sqrt(spread + EPSILON) * gain_ref[...]
    out_ref[...] = gelu(normal).astype(BF16)


def head_kernel(
    pair_ref, mid_ref, far_ref, weight_ref, bias_ref, class_ref, class_bias_ref, labels_ref,
    logits_ref, losses_ref, sum_ref, act,
):
    _, place = positions()
    strip = 2
    odd = lax.rem(place, 2)
    edge = 2 * strip * COLS
    act[pl.ds(pl.multiple_of((1 - odd) * edge, strip * COLS), strip * COLS), :] = pair_ref[...]
    act[strip * COLS : edge, :] = mid_ref[...]
    act[pl.ds(pl.multiple_of(odd * edge, strip * COLS), strip * COLS), :] = far_ref[...]
    count = (strip + 2) * COLS
    stacked = jnp.concatenate([act[r * COLS : r * COLS + count] for r in range(3)], axis=1)
    products = []
    for s in range(3):
        weight = jnp.concatenate([weight_ref[3 * r + s] for r in range(3)], axis=0)
        products.append(jnp.dot(stacked, weight, preferred_element_type=F32))
    position = lax.broadcasted_iota(jnp.int32, (count, CHANNELS), 0)
    col = position % COLS
    total = products[1]
    total = total + jnp.where(col == 0, 0.0, pltpu.roll(products[0], 1, 0))
    total = total + jnp.where(col == COLS - 1, 0.0, pltpu.roll(products[2], count - 1, 0))
    hidden = gelu(total + bias_ref[...])
    grid_row = place * strip - 1 + position // COLS
    inside = (grid_row >= 0) & (grid_row < strip * SEQ)
    hidden = jnp.where(inside, hidden, 0.0).astype(BF16)

    taps = lax.dot_general(
        class_ref[...], hidden, (((1,), (1,)), ((), ())), preferred_element_type=F32
    )

    def tap(r, s, row):
        start = (3 * r + s) * CLASSES
        return taps[start : start + CLASSES, row * COLS : (row + 1) * COLS]

    sides = []
    for s in range(3):
        combos = []
        for row in (1, 2):
            t = [tap(r, s, row) for r in range(3)]
            combos.append(tap(0, s, row - 1) + t[1] + t[2])
            combos.append(t[0] + t[1] + t[2])
            combos.append(t[0] + t[1] + tap(2, s, row + 1))
        sides.append(jnp.concatenate(combos, axis=0))
    pixels = UPSCALE * COLS
    source = lax.broadcasted_iota(jnp.int32, (COLS, pixels), 0)
    target = lax.broadcasted_iota(jnp.int32, (COLS, pixels), 1)
    spread_sum = None
    for s, side in enumerate(sides):
        first = UPSCALE * source - s + 1
        expand = jnp.where((target >= first) & (target < first + UPSCALE), 1.0, 0.0).astype(BF16)
        parts = []
        for _ in range(3):
            parts.append(side.astype(BF16))
            side = side - parts[-1].astype(F32)
        terms = jnp.dot(jnp.concatenate(parts, axis=0), expand, preferred_element_type=F32)
        count = side.shape[0]
        term = terms[:count] + terms[count : 2 * count] + terms[2 * count :]
        spread_sum = term if spread_sum is None else spread_sum + term
    class_ids = lax.broadcasted_iota(jnp.int32, (CLASSES, pixels), 0)
    loss_sum = jnp.zeros((1, pixels), F32)
    for combo in range(3 * strip):
        logits = spread_sum[combo * CLASSES : (combo + 1) * CLASSES] + class_bias_ref[...]
        highest = jnp.max(logits, axis=0, keepdims=True)
        log_total = highest + jnp.log(jnp.sum(jnp.exp(logits - highest), axis=0, keepdims=True))
        for inner in ((0,), (1, 2), (3,))[combo % 3]:
            y = UPSCALE * (combo // 3) + inner
            logits_ref[:, y, :] = logits
            chosen = class_ids == labels_ref[y : y + 1, :]
            picked = jnp.sum(jnp.where(chosen, logits, 0.0), axis=0, keepdims=True)
            loss = log_total - picked
            losses_ref[y : y + 1, :] = loss
            loss_sum = loss_sum + loss
    total_loss = jnp.sum(loss_sum, axis=1, keepdims=True) * (1.0 / (SEQ * losses_ref.size))
    sum_ref[...] = jnp.broadcast_to(total_loss[None], sum_ref.shape)


def body(
    mesh_shape, queries, keys, values, proj_weight, norm_gain, conv_weight, conv_bias, class_weight,
    class_bias, labels,
):
    cosine, sine = rotary_tables()
    crops = mesh_shape["crop"]
    seq = ("y", "z")

    swaps = []
    for crop in range(crops):
        for y in range(YS):
            slot = (y - crop % 2) % YS
            swaps.append((crop * YS + y, crop * YS + ((slot ^ 1) + crop % 2) % YS))

    send = pack(queries, keys, values, cosine, sine).reshape(SEQ, 3 * COLS, HEAD_DIM)
    mine = lax.all_to_all(send, seq, 0, 0, tiled=True)
    attended = attend(mine, lambda x: lax.ppermute(x, ("crop", "y"), swaps))
    returned = lax.all_to_all(attended, seq, 0, 0, tiled=True)

    strip_tokens = queries.shape[0]
    act = pl.pallas_call(
        features_kernel,
        in_specs=[VMEM] * 3,
        out_specs=VMEM,
        out_shape=jax.ShapeDtypeStruct((strip_tokens, CHANNELS), BF16),
        compiler_params=limit(12),
        name="features",
    )(returned, proj_weight, norm_gain.reshape(1, CHANNELS))
    far = lax.ppermute(act, seq, [(i, ((i + 1) ^ 1) - 1) for i in range(1, SEQ - 1)])
    pair = lax.ppermute(act, seq, [(i, i ^ 1) for i in range(SEQ)])
    rows, pixels = labels.shape
    logits, losses, sums = pl.pallas_call(
        head_kernel,
        in_specs=[VMEM] * 8,
        out_specs=[VMEM] * 3,
        out_shape=[
            jax.ShapeDtypeStruct((CLASSES, rows, pixels), F32),
            jax.ShapeDtypeStruct((rows, pixels), F32),
            jax.ShapeDtypeStruct((SEQ, 1, HEAD_DIM), F32),
        ],
        scratch_shapes=[pltpu.VMEM((3 * strip_tokens, CHANNELS), BF16)],
        compiler_params=limit(12),
        name="head",
    )(
        pair, act, far, conv_weight, conv_bias.reshape(1, CHANNELS),
        class_weight.reshape(9 * CLASSES, CHANNELS), class_bias.reshape(CLASSES, 1), labels,
    )
    everyone = lax.all_to_all(sums, seq, 0, 0, tiled=True)
    loss = jnp.sum(everyone[:, 0, 0]).reshape(1)
    return logits, losses, loss


def solution(mesh):
    crops = mesh.shape["crop"]
    split = Mesh(mesh.devices.reshape(crops, YS, ZS), ("crop", "y", "z"))
    rows = P(("crop", "y", "z"), None)
    in_specs = (rows, rows, rows, P(), P(), P(), P(), P(), P(), rows)
    out_specs = (P(None, ("crop", "y", "z"), None), rows, P("crop"))
    return jax.shard_map(
        functools.partial(body, dict(split.shape)),
        mesh=split,
        in_specs=in_specs,
        out_specs=out_specs,
        check_vma=False,
    )
```

```python
import functools
import math

import jax
import jax.numpy as jnp
import numpy as np
from jax import lax
from jax.experimental import pallas as pl
from jax.experimental.pallas import tpu as pltpu
from jax.sharding import Mesh, PartitionSpec as P


HEADS = 16
HEAD_DIM = 128
UPSCALE = 4
COLS = 64
CHANNELS = 256
CLASSES = 16
YS = 4
ZS = 8
SEQ = YS * ZS
EPSILON = 1e-05
EXP_SCALE = HEAD_DIM**-0.5 * math.log2(math.e)
VMEM = pl.BlockSpec(memory_space=pltpu.VMEM)
BF16 = jnp.bfloat16
F32 = jnp.float32


def limit(mib):
    return pltpu.CompilerParams(vmem_limit_bytes=mib << 20)


def rotary_tables():
    quarter = HEAD_DIM // 4
    omegas = np.power(np.float32(100.0), -np.arange(quarter, dtype=np.float32) / np.float32(quarter))
    angles = np.arange(COLS, dtype=np.float32)[:, None] * omegas[None, :].astype(np.float32)
    cosine = np.cos(angles).astype(np.float32)
    sine = np.sin(angles).astype(np.float32)
    wide_cos = np.concatenate([cosine] * 4, axis=1)
    wide_sin = np.concatenate([-sine, sine, -sine, sine], axis=1)
    return wide_cos, wide_sin


def gelu(x):
    return x * (0.5 * (1.0 + lax.erf(x * np.float32(math.sqrt(0.5)))))


def positions():
    place = lax.axis_index("y") * ZS + lax.axis_index("z")
    return lax.rem(lax.axis_index("crop"), 2), place


HALVES = 2


def pack_kernel(q_hbm, k_hbm, v_hbm, cos_hbm, sin_hbm, out_ref, q_ref, k_ref, v_ref, cos_ref, sin_ref, sems, table_sems):
    core, place = positions()
    tables_in = [
        pltpu.make_async_copy(cos_hbm, cos_ref, table_sems.at[0]),
        pltpu.make_async_copy(sin_hbm, sin_ref, table_sems.at[1]),
    ]
    copies = []
    for half in range(HALVES):
        rows = pl.ds(half * COLS, COLS)
        copies.append(
            [
                pltpu.make_async_copy(hbm.at[rows], ref.at[rows], sems.at[half, which])
                for which, (hbm, ref) in enumerate(((q_hbm, q_ref), (k_hbm, k_ref), (v_hbm, v_ref)))
            ]
        )
        for copy in copies[-1]:
            copy.start()
        if half == 0:
            for copy in tables_in:
                copy.start()
    lane = lax.broadcasted_iota(jnp.int32, (COLS, HEAD_DIM), 1)
    by_row = lane < HEAD_DIM // 2
    first = (lane % (HEAD_DIM // 2)) < HEAD_DIM // 4
    for copy in tables_in:
        copy.wait()
    for half in range(HALVES):
        row = pl.ds(2 * place + half, 1)
        cosine, sine = [
            jnp.where(by_row, ref[row, :], ref[...]) for ref in (cos_ref, sin_ref)
        ]
        rows = slice(half * COLS, (half + 1) * COLS)
        for index, ref in ((0, q_ref), (1, k_ref), (2, v_ref)):
            copies[half][index].wait()
            for head in range(HEADS):
                y = lax.rem(2 * (head % 2) + half + core, YS)
                x = ref[rows, head * HEAD_DIM : (head + 1) * HEAD_DIM]
                if index < 2:
                    x = x.astype(F32)
                    partner = jnp.where(
                        first,
                        pltpu.roll(x, HEAD_DIM - HEAD_DIM // 4, 1),
                        pltpu.roll(x, HEAD_DIM // 4, 1),
                    )
                    x = (x * cosine + partner * sine).astype(BF16)
                out_ref[y, head // 2, index * COLS : (index + 1) * COLS, :] = x


def pack(queries, keys, values, cosine, sine):
    return pl.pallas_call(
        pack_kernel,
        in_specs=[pl.BlockSpec(memory_space=pltpu.HBM)] * 5,
        out_specs=VMEM,
        out_shape=jax.ShapeDtypeStruct((YS, ZS, 3 * COLS, HEAD_DIM), BF16),
        scratch_shapes=[pltpu.VMEM(queries.shape, BF16)] * 3
        + [pltpu.VMEM((COLS, HEAD_DIM), F32)] * 2
        + [pltpu.SemaphoreType.DMA((HALVES, 3)), pltpu.SemaphoreType.DMA((2,))],
        compiler_params=limit(8),
        name="pack",
    )(*(pltpu.with_memory_space_constraint(x, pltpu.HBM) for x in (queries, keys, values, cosine, sine)))


BLOCK = 4


def scores_of(query, key):
    return lax.dot_general(query, key, (((1,), (1,)), ((), ())), preferred_element_type=F32)


def with_ones(value):
    return jnp.concatenate([value, jnp.ones_like(value)], axis=1)


OWN_CHUNK = 512
MORE_CHUNK = 256
LAST_CHUNK = 768


def sweep(query, key, value, chunk):
    top = total = None
    for start in range(0, key.shape[0], chunk):
        scores = scores_of(query, key[start : start + chunk])
        before, top = top, jnp.max(scores, axis=1, keepdims=True)
        if before is not None:
            top = jnp.maximum(before, top)
        weights = jnp.exp2((scores - top) * EXP_SCALE).astype(BF16)
        part = jnp.dot(weights, value[start : start + chunk], preferred_element_type=F32)
        total = part if before is None else total * jnp.exp2((before - top) * EXP_SCALE) + part
    return jnp.broadcast_to(top, (query.shape[0], HEAD_DIM)), total


def keys_values(ref, first):
    tokens = ref.shape[0] * COLS
    key = ref[:, first : first + COLS, :].reshape(tokens, HEAD_DIM)
    value = ref[:, first + COLS : first + 2 * COLS, :].reshape(tokens, HEAD_DIM)
    return key, with_ones(value)


def each_block(visit):
    def step(i, carry):
        rows = BLOCK * COLS
        visit(pl.ds(i * BLOCK, BLOCK), pl.ds(pl.multiple_of(i * rows, rows), rows))
        return carry

    lax.fori_loop(0, SEQ // BLOCK, step, 0, unroll=SEQ // BLOCK)


def joined(one, two):
    top = jnp.maximum(one[0], two[0])
    fades = [jnp.exp2((side[0] - top) * EXP_SCALE) for side in (one, two)]
    mixed, norm = [
        one[1][:, lanes] * fades[0] + two[1][:, lanes] * fades[1]
        for lanes in (slice(0, HEAD_DIM), slice(HEAD_DIM, 2 * HEAD_DIM))
    ]
    return top, mixed, norm


def own_kernel(mine_ref, acc_ref, top_ref):
    key, value = keys_values(mine_ref, COLS)

    def visit(block, rows):
        query = mine_ref[block, :COLS, :].reshape(BLOCK * COLS, HEAD_DIM)
        top_ref[rows, :], acc_ref[rows, :] = sweep(query, key, value, OWN_CHUNK)

    each_block(visit)


def more_kernel(mine_ref, other_ref, acc_ref, top_ref, new_acc_ref, new_top_ref):
    key, value = keys_values(other_ref, 0)

    def visit(block, rows):
        query = mine_ref[block, :COLS, :].reshape(BLOCK * COLS, HEAD_DIM)
        top, mixed, norm = joined(sweep(query, key, value, MORE_CHUNK), (top_ref[rows, :], acc_ref[rows, :]))
        new_top_ref[rows, :] = top
        new_acc_ref[rows, :HEAD_DIM] = mixed
        new_acc_ref[rows, HEAD_DIM:] = norm

    each_block(visit)


def last_kernel(mine_ref, other_ref, acc_ref, top_ref, out_ref):
    key, value = keys_values(other_ref, 0)

    def visit(block, rows):
        query = mine_ref[block, :COLS, :].reshape(BLOCK * COLS, HEAD_DIM)
        _, mixed, norm = joined(sweep(query, key, value, LAST_CHUNK), (top_ref[rows, :], acc_ref[rows, :]))
        out_ref[block, :, :] = (mixed / norm).astype(BF16).reshape(BLOCK, COLS, HEAD_DIM)

    each_block(visit)


FIRST = 20


def attend(mine, swap):
    tokens = SEQ * COLS

    def cost(sources):
        pairs = tokens * sources * COLS
        return pl.CostEstimate(flops=6 * pairs * HEAD_DIM, bytes_accessed=4 << 20, transcendentals=pairs)

    running = [
        jax.ShapeDtypeStruct((tokens, 2 * HEAD_DIM), F32),
        jax.ShapeDtypeStruct((tokens, HEAD_DIM), F32),
    ]
    one = swap(mine[:FIRST, COLS:, :])
    two = swap(mine[FIRST:, COLS:, :])
    acc, top = pl.pallas_call(
        own_kernel,
        in_specs=[VMEM],
        out_specs=[VMEM, VMEM],
        out_shape=running,
        cost_estimate=cost(SEQ),
        compiler_params=limit(28),
        name="own_keys",
    )(mine)
    acc, top = pl.pallas_call(
        more_kernel,
        in_specs=[VMEM] * 4,
        out_specs=[VMEM, VMEM],
        out_shape=running,
        cost_estimate=cost(FIRST),
        compiler_params=limit(28),
        name="more_keys",
    )(mine, one, acc, top)
    return pl.pallas_call(
        last_kernel,
        in_specs=[VMEM] * 4,
        out_specs=VMEM,
        out_shape=jax.ShapeDtypeStruct((SEQ, COLS, HEAD_DIM), BF16),
        cost_estimate=cost(SEQ - FIRST),
        compiler_params=limit(28),
        name="last_keys",
    )(mine, two, acc, top)


def features_kernel(mixed_ref, proj_ref, gain_ref, out_ref):
    core, _ = positions()
    strips = []
    for half in range(2):
        pieces = []
        for head in range(HEADS):
            y = lax.rem(2 * (head % 2) + half + core, YS)
            pieces.append(mixed_ref[y * ZS + head // 2])
        strips.append(jnp.concatenate(pieces, axis=1))
    mixed = jnp.concatenate(strips, axis=0)
    features = jnp.dot(mixed, proj_ref[...], preferred_element_type=F32)
    center = jnp.mean(features, axis=-1, keepdims=True)
    spread = jnp.mean((features - center) ** 2, axis=-1, keepdims=True)
    normal = (features - center) / jnp.sqrt(spread + EPSILON) * gain_ref[...]
    out_ref[...] = gelu(normal).astype(BF16)


def head_kernel(
    pair_ref, mid_ref, far_ref, weight_ref, bias_ref, class_ref, class_bias_ref, labels_ref,
    logits_ref, losses_ref, sum_ref, act,
):
    _, place = positions()
    strip = 2
    odd = lax.rem(place, 2)
    edge = 2 * strip * COLS
    act[pl.ds(pl.multiple_of((1 - odd) * edge, strip * COLS), strip * COLS), :] = pair_ref[...]
    act[strip * COLS : edge, :] = mid_ref[...]
    act[pl.ds(pl.multiple_of(odd * edge, strip * COLS), strip * COLS), :] = far_ref[...]
    count = (strip + 2) * COLS
    stacked = jnp.concatenate([act[r * COLS : r * COLS + count] for r in range(3)], axis=1)
    products = []
    for s in range(3):
        weight = jnp.concatenate([weight_ref[3 * r + s] for r in range(3)], axis=0)
        products.append(jnp.dot(stacked, weight, preferred_element_type=F32))
    position = lax.broadcasted_iota(jnp.int32, (count, CHANNELS), 0)
    col = position % COLS
    total = products[1]
    total = total + jnp.where(col == 0, 0.0, pltpu.roll(products[0], 1, 0))
    total = total + jnp.where(col == COLS - 1, 0.0, pltpu.roll(products[2], count - 1, 0))
    hidden = gelu(total + bias_ref[...])
    grid_row = place * strip - 1 + position // COLS
    inside = (grid_row >= 0) & (grid_row < strip * SEQ)
    hidden = jnp.where(inside, hidden, 0.0).astype(BF16)

    taps = lax.dot_general(
        class_ref[...], hidden, (((1,), (1,)), ((), ())), preferred_element_type=F32
    )

    def tap(r, s, row):
        start = (3 * r + s) * CLASSES
        return taps[start : start + CLASSES, row * COLS : (row + 1) * COLS]

    sides = []
    for s in range(3):
        combos = []
        for row in (1, 2):
            t = [tap(r, s, row) for r in range(3)]
            combos.append(tap(0, s, row - 1) + t[1] + t[2])
            combos.append(t[0] + t[1] + t[2])
            combos.append(t[0] + t[1] + tap(2, s, row + 1))
        sides.append(jnp.concatenate(combos, axis=0))
    pixels = UPSCALE * COLS
    source = lax.broadcasted_iota(jnp.int32, (COLS, pixels), 0)
    target = lax.broadcasted_iota(jnp.int32, (COLS, pixels), 1)
    spread_sum = None
    for s, side in enumerate(sides):
        first = UPSCALE * source - s + 1
        expand = jnp.where((target >= first) & (target < first + UPSCALE), 1.0, 0.0).astype(BF16)
        parts = []
        for _ in range(3):
            parts.append(side.astype(BF16))
            side = side - parts[-1].astype(F32)
        terms = jnp.dot(jnp.concatenate(parts, axis=0), expand, preferred_element_type=F32)
        count = side.shape[0]
        term = terms[:count] + terms[count : 2 * count] + terms[2 * count :]
        spread_sum = term if spread_sum is None else spread_sum + term
    class_ids = lax.broadcasted_iota(jnp.int32, (CLASSES, pixels), 0)
    loss_sum = jnp.zeros((1, pixels), F32)
    for combo in range(3 * strip):
        logits = spread_sum[combo * CLASSES : (combo + 1) * CLASSES] + class_bias_ref[...]
        highest = jnp.max(logits, axis=0, keepdims=True)
        log_total = highest + jnp.log(jnp.sum(jnp.exp(logits - highest), axis=0, keepdims=True))
        for inner in ((0,), (1, 2), (3,))[combo % 3]:
            y = UPSCALE * (combo // 3) + inner
            logits_ref[:, y, :] = logits
            chosen = class_ids == labels_ref[y : y + 1, :]
            picked = jnp.sum(jnp.where(chosen, logits, 0.0), axis=0, keepdims=True)
            loss = log_total - picked
            losses_ref[y : y + 1, :] = loss
            loss_sum = loss_sum + loss
    total_loss = jnp.sum(loss_sum, axis=1, keepdims=True) * (1.0 / (SEQ * losses_ref.size))
    sum_ref[...] = jnp.broadcast_to(total_loss[None], sum_ref.shape)


def body(
    mesh_shape, queries, keys, values, proj_weight, norm_gain, conv_weight, conv_bias, class_weight,
    class_bias, labels,
):
    cosine, sine = rotary_tables()
    crops = mesh_shape["crop"]
    seq = ("y", "z")

    swaps = []
    for crop in range(crops):
        for y in range(YS):
            slot = (y - crop % 2) % YS
            swaps.append((crop * YS + y, crop * YS + ((slot ^ 1) + crop % 2) % YS))

    send = pack(queries, keys, values, cosine, sine).reshape(SEQ, 3 * COLS, HEAD_DIM)
    mine = lax.all_to_all(send, seq, 0, 0, tiled=True)
    attended = attend(mine, lambda x: lax.ppermute(x, ("crop", "y"), swaps))
    returned = lax.all_to_all(attended, seq, 0, 0, tiled=True)

    strip_tokens = queries.shape[0]
    act = pl.pallas_call(
        features_kernel,
        in_specs=[VMEM] * 3,
        out_specs=VMEM,
        out_shape=jax.ShapeDtypeStruct((strip_tokens, CHANNELS), BF16),
        compiler_params=limit(12),
        name="features",
    )(returned, proj_weight, norm_gain.reshape(1, CHANNELS))
    far = lax.ppermute(act, seq, [(i, ((i + 1) ^ 1) - 1) for i in range(1, SEQ - 1)])
    pair = lax.ppermute(act, seq, [(i, i ^ 1) for i in range(SEQ)])
    rows, pixels = labels.shape
    logits, losses, sums = pl.pallas_call(
        head_kernel,
        in_specs=[VMEM] * 8,
        out_specs=[VMEM] * 3,
        out_shape=[
            jax.ShapeDtypeStruct((CLASSES, rows, pixels), F32),
            jax.ShapeDtypeStruct((rows, pixels), F32),
            jax.ShapeDtypeStruct((SEQ, 1, HEAD_DIM), F32),
        ],
        scratch_shapes=[pltpu.VMEM((3 * strip_tokens, CHANNELS), BF16)],
        compiler_params=limit(12),
        name="head",
    )(
        pair, act, far, conv_weight, conv_bias.reshape(1, CHANNELS),
        class_weight.reshape(9 * CLASSES, CHANNELS), class_bias.reshape(CLASSES, 1), labels,
    )
    everyone = lax.all_to_all(sums, seq, 0, 0, tiled=True)
    loss = jnp.sum(everyone, axis=(0, 1))[:1]
    return logits, losses, loss


def solution(mesh):
    crops = mesh.shape["crop"]
    split = Mesh(mesh.devices.reshape(crops, YS, ZS), ("crop", "y", "z"))
    rows = P(("crop", "y", "z"), None)
    in_specs = (rows, rows, rows, P(), P(), P(), P(), P(), P(), rows)
    out_specs = (P(None, ("crop", "y", "z"), None), rows, P("crop"))
    return jax.shard_map(
        functools.partial(body, dict(split.shape)),
        mesh=split,
        in_specs=in_specs,
        out_specs=out_specs,
        check_vma=False,
    )
```

```python
import functools
import math

import jax
import jax.numpy as jnp
import numpy as np
from jax import lax
from jax.experimental import pallas as pl
from jax.experimental.pallas import tpu as pltpu
from jax.sharding import Mesh, PartitionSpec as P


HEADS = 16
HEAD_DIM = 128
UPSCALE = 4
COLS = 64
CHANNELS = 256
CLASSES = 16
YS = 4
ZS = 8
SEQ = YS * ZS
EPSILON = 1e-05
EXP_SCALE = HEAD_DIM**-0.5 * math.log2(math.e)
VMEM = pl.BlockSpec(memory_space=pltpu.VMEM)
BF16 = jnp.bfloat16
F32 = jnp.float32


def limit(mib):
    return pltpu.CompilerParams(vmem_limit_bytes=mib << 20)


def rotary_tables():
    quarter = HEAD_DIM // 4
    omegas = np.power(np.float32(100.0), -np.arange(quarter, dtype=np.float32) / np.float32(quarter))
    angles = np.arange(COLS, dtype=np.float32)[:, None] * omegas[None, :].astype(np.float32)
    cosine = np.cos(angles).astype(np.float32)
    sine = np.sin(angles).astype(np.float32)
    wide_cos = np.concatenate([cosine] * 4, axis=1)
    wide_sin = np.concatenate([-sine, sine, -sine, sine], axis=1)
    return wide_cos, wide_sin


def gelu(x):
    return x * (0.5 * (1.0 + lax.erf(x * np.float32(math.sqrt(0.5)))))


def positions():
    place = lax.axis_index("y") * ZS + lax.axis_index("z")
    return lax.rem(lax.axis_index("crop"), 2), place


HALVES = 2


def pack_kernel(q_hbm, k_hbm, v_hbm, cos_hbm, sin_hbm, out_ref, q_ref, k_ref, v_ref, cos_ref, sin_ref, sems, table_sems):
    core, place = positions()
    tables_in = [
        pltpu.make_async_copy(cos_hbm, cos_ref, table_sems.at[0]),
        pltpu.make_async_copy(sin_hbm, sin_ref, table_sems.at[1]),
    ]
    copies = []
    for half in range(HALVES):
        rows = pl.ds(half * COLS, COLS)
        copies.append(
            [
                pltpu.make_async_copy(hbm.at[rows], ref.at[rows], sems.at[half, which])
                for which, (hbm, ref) in enumerate(((q_hbm, q_ref), (k_hbm, k_ref), (v_hbm, v_ref)))
            ]
        )
        for copy in copies[-1]:
            copy.start()
        if half == 0:
            for copy in tables_in:
                copy.start()
    lane = lax.broadcasted_iota(jnp.int32, (COLS, HEAD_DIM), 1)
    by_row = lane < HEAD_DIM // 2
    first = (lane % (HEAD_DIM // 2)) < HEAD_DIM // 4
    for copy in tables_in:
        copy.wait()
    for half in range(HALVES):
        row = pl.ds(2 * place + half, 1)
        cosine, sine = [
            jnp.where(by_row, ref[row, :], ref[...]) for ref in (cos_ref, sin_ref)
        ]
        rows = slice(half * COLS, (half + 1) * COLS)
        for index, ref in ((0, q_ref), (1, k_ref), (2, v_ref)):
            copies[half][index].wait()
            for head in range(HEADS):
                y = lax.rem(2 * (head % 2) + half + core, YS)
                x = ref[rows, head * HEAD_DIM : (head + 1) * HEAD_DIM]
                if index < 2:
                    x = x.astype(F32)
                    partner = jnp.where(
                        first,
                        pltpu.roll(x, HEAD_DIM - HEAD_DIM // 4, 1),
                        pltpu.roll(x, HEAD_DIM // 4, 1),
                    )
                    x = (x * cosine + partner * sine).astype(BF16)
                out_ref[y, head // 2, index * COLS : (index + 1) * COLS, :] = x


def pack(queries, keys, values, cosine, sine):
    return pl.pallas_call(
        pack_kernel,
        in_specs=[pl.BlockSpec(memory_space=pltpu.HBM)] * 5,
        out_specs=VMEM,
        out_shape=jax.ShapeDtypeStruct((YS, ZS, 3 * COLS, HEAD_DIM), BF16),
        scratch_shapes=[pltpu.VMEM(queries.shape, BF16)] * 3
        + [pltpu.VMEM((COLS, HEAD_DIM), F32)] * 2
        + [pltpu.SemaphoreType.DMA((HALVES, 3)), pltpu.SemaphoreType.DMA((2,))],
        compiler_params=limit(8),
        name="pack",
    )(*(pltpu.with_memory_space_constraint(x, pltpu.HBM) for x in (queries, keys, values, cosine, sine)))


BLOCK = 4


def scores_of(query, key):
    return lax.dot_general(query, key, (((1,), (1,)), ((), ())), preferred_element_type=F32)


def with_ones(value):
    return jnp.concatenate([value, jnp.ones_like(value)], axis=1)


OWN_CHUNK = 512
MORE_CHUNK = 256
LAST_CHUNK = 768


def sweep(query, key, value, chunk):
    top = total = None
    for start in range(0, key.shape[0], chunk):
        scores = scores_of(query, key[start : start + chunk])
        before, top = top, jnp.max(scores, axis=1, keepdims=True)
        if before is not None:
            top = jnp.maximum(before, top)
        weights = jnp.exp2((scores - top) * EXP_SCALE).astype(BF16)
        part = jnp.dot(weights, value[start : start + chunk], preferred_element_type=F32)
        total = part if before is None else total * jnp.exp2((before - top) * EXP_SCALE) + part
    return jnp.broadcast_to(top, (query.shape[0], HEAD_DIM)), total


def keys_values(ref, first):
    tokens = ref.shape[0] * COLS
    key = ref[:, first : first + COLS, :].reshape(tokens, HEAD_DIM)
    value = ref[:, first + COLS : first + 2 * COLS, :].reshape(tokens, HEAD_DIM)
    return key, with_ones(value)


def each_block(visit):
    def step(i, carry):
        rows = BLOCK * COLS
        visit(pl.ds(i * BLOCK, BLOCK), pl.ds(pl.multiple_of(i * rows, rows), rows))
        return carry

    lax.fori_loop(0, SEQ // BLOCK, step, 0, unroll=SEQ // BLOCK)


def joined(one, two):
    top = jnp.maximum(one[0], two[0])
    fades = [jnp.exp2((side[0] - top) * EXP_SCALE) for side in (one, two)]
    mixed, norm = [
        one[1][:, lanes] * fades[0] + two[1][:, lanes] * fades[1]
        for lanes in (slice(0, HEAD_DIM), slice(HEAD_DIM, 2 * HEAD_DIM))
    ]
    return top, mixed, norm


def own_kernel(mine_ref, acc_ref, top_ref):
    key, value = keys_values(mine_ref, COLS)

    def visit(block, rows):
        query = mine_ref[block, :COLS, :].reshape(BLOCK * COLS, HEAD_DIM)
        top_ref[rows, :], acc_ref[rows, :] = sweep(query, key, value, OWN_CHUNK)

    each_block(visit)


def more_kernel(mine_ref, other_ref, acc_ref, top_ref, new_acc_ref, new_top_ref):
    key, value = keys_values(other_ref, 0)

    def visit(block, rows):
        query = mine_ref[block, :COLS, :].reshape(BLOCK * COLS, HEAD_DIM)
        top, mixed, norm = joined(sweep(query, key, value, MORE_CHUNK), (top_ref[rows, :], acc_ref[rows, :]))
        new_top_ref[rows, :] = top
        new_acc_ref[rows, :HEAD_DIM] = mixed
        new_acc_ref[rows, HEAD_DIM:] = norm

    each_block(visit)


def last_kernel(mine_ref, other_ref, acc_ref, top_ref, out_ref):
    key, value = keys_values(other_ref, 0)

    def visit(block, rows):
        query = mine_ref[block, :COLS, :].reshape(BLOCK * COLS, HEAD_DIM)
        _, mixed, norm = joined(sweep(query, key, value, LAST_CHUNK), (top_ref[rows, :], acc_ref[rows, :]))
        out_ref[block, :, :] = (mixed / norm).astype(BF16).reshape(BLOCK, COLS, HEAD_DIM)

    each_block(visit)


FIRST = 20


def attend(mine, swap):
    tokens = SEQ * COLS

    def cost(sources):
        pairs = tokens * sources * COLS
        return pl.CostEstimate(flops=6 * pairs * HEAD_DIM, bytes_accessed=4 << 20, transcendentals=pairs)

    running = [
        jax.ShapeDtypeStruct((tokens, 2 * HEAD_DIM), F32),
        jax.ShapeDtypeStruct((tokens, HEAD_DIM), F32),
    ]
    one = swap(mine[:FIRST, COLS:, :])
    two = swap(mine[FIRST:, COLS:, :])
    acc, top = pl.pallas_call(
        own_kernel,
        in_specs=[VMEM],
        out_specs=[VMEM, VMEM],
        out_shape=running,
        cost_estimate=cost(SEQ),
        compiler_params=limit(28),
        name="own_keys",
    )(mine)
    acc, top = pl.pallas_call(
        more_kernel,
        in_specs=[VMEM] * 4,
        out_specs=[VMEM, VMEM],
        out_shape=running,
        cost_estimate=cost(FIRST),
        compiler_params=limit(28),
        name="more_keys",
    )(mine, one, acc, top)
    return pl.pallas_call(
        last_kernel,
        in_specs=[VMEM] * 4,
        out_specs=VMEM,
        out_shape=jax.ShapeDtypeStruct((SEQ, COLS, HEAD_DIM), BF16),
        cost_estimate=cost(SEQ - FIRST),
        compiler_params=limit(28),
        name="last_keys",
    )(mine, two, acc, top)


def features_kernel(mixed_ref, proj_ref, gain_ref, out_ref):
    core, _ = positions()
    strips = []
    for half in range(2):
        pieces = []
        for head in range(HEADS):
            y = lax.rem(2 * (head % 2) + half + core, YS)
            pieces.append(mixed_ref[y * ZS + head // 2])
        strips.append(jnp.concatenate(pieces, axis=1))
    mixed = jnp.concatenate(strips, axis=0)
    features = jnp.dot(mixed, proj_ref[...], preferred_element_type=F32)
    center = jnp.mean(features, axis=-1, keepdims=True)
    spread = jnp.mean((features - center) ** 2, axis=-1, keepdims=True)
    normal = (features - center) / jnp.sqrt(spread + EPSILON) * gain_ref[...]
    out_ref[...] = gelu(normal).astype(BF16)


def head_kernel(
    pair_ref, mid_ref, far_ref, weight_ref, bias_ref, class_ref, class_bias_ref, labels_ref,
    logits_ref, losses_ref, sum_ref, act,
):
    _, place = positions()
    strip = 2
    odd = lax.rem(place, 2)
    edge = 2 * strip * COLS
    act[pl.ds(pl.multiple_of((1 - odd) * edge, strip * COLS), strip * COLS), :] = pair_ref[...]
    act[strip * COLS : edge, :] = mid_ref[...]
    act[pl.ds(pl.multiple_of(odd * edge, strip * COLS), strip * COLS), :] = far_ref[...]
    count = (strip + 2) * COLS
    stacked = jnp.concatenate([act[r * COLS : r * COLS + count] for r in range(3)], axis=1)
    products = []
    for s in range(3):
        weight = jnp.concatenate([weight_ref[3 * r + s] for r in range(3)], axis=0)
        products.append(jnp.dot(stacked, weight, preferred_element_type=F32))
    position = lax.broadcasted_iota(jnp.int32, (count, CHANNELS), 0)
    col = position % COLS
    total = products[1]
    total = total + jnp.where(col == 0, 0.0, pltpu.roll(products[0], 1, 0))
    total = total + jnp.where(col == COLS - 1, 0.0, pltpu.roll(products[2], count - 1, 0))
    hidden = gelu(total + bias_ref[...])
    grid_row = place * strip - 1 + position // COLS
    inside = (grid_row >= 0) & (grid_row < strip * SEQ)
    hidden = jnp.where(inside, hidden, 0.0).astype(BF16)

    taps = lax.dot_general(
        class_ref[...], hidden, (((1,), (1,)), ((), ())), preferred_element_type=F32
    )

    def tap(r, s, row):
        start = (3 * r + s) * CLASSES
        return taps[start : start + CLASSES, row * COLS : (row + 1) * COLS]

    sides = []
    for s in range(3):
        combos = []
        for row in (1, 2):
            t = [tap(r, s, row) for r in range(3)]
            combos.append(tap(0, s, row - 1) + t[1] + t[2])
            combos.append(t[0] + t[1] + t[2])
            combos.append(t[0] + t[1] + tap(2, s, row + 1))
        sides.append(jnp.concatenate(combos, axis=0))
    pixels = UPSCALE * COLS
    source = lax.broadcasted_iota(jnp.int32, (COLS, pixels), 0)
    target = lax.broadcasted_iota(jnp.int32, (COLS, pixels), 1)
    spread_sum = None
    for s, side in enumerate(sides):
        first = UPSCALE * source - s + 1
        expand = jnp.where((target >= first) & (target < first + UPSCALE), 1.0, 0.0).astype(BF16)
        parts = []
        for _ in range(3):
            parts.append(side.astype(BF16))
            side = side - parts[-1].astype(F32)
        terms = jnp.dot(jnp.concatenate(parts, axis=0), expand, preferred_element_type=F32)
        count = side.shape[0]
        term = terms[:count] + terms[count : 2 * count] + terms[2 * count :]
        spread_sum = term if spread_sum is None else spread_sum + term
    class_ids = lax.broadcasted_iota(jnp.int32, (CLASSES, pixels), 0)
    loss_sum = jnp.zeros((1, pixels), F32)
    for combo in range(3 * strip):
        logits = spread_sum[combo * CLASSES : (combo + 1) * CLASSES] + class_bias_ref[...]
        highest = jnp.max(logits, axis=0, keepdims=True)
        log_total = highest + jnp.log(jnp.sum(jnp.exp(logits - highest), axis=0, keepdims=True))
        for inner in ((0,), (1, 2), (3,))[combo % 3]:
            y = UPSCALE * (combo // 3) + inner
            logits_ref[:, y, :] = logits
            chosen = class_ids == labels_ref[y : y + 1, :]
            picked = jnp.sum(jnp.where(chosen, logits, 0.0), axis=0, keepdims=True)
            loss = log_total - picked
            losses_ref[y : y + 1, :] = loss
            loss_sum = loss_sum + loss
    total_loss = jnp.sum(loss_sum, axis=1, keepdims=True) * (1.0 / (SEQ * losses_ref.size))
    sum_ref[...] = jnp.broadcast_to(total_loss[None], sum_ref.shape)


def body(
    mesh_shape, queries, keys, values, proj_weight, norm_gain, conv_weight, conv_bias, class_weight,
    class_bias, labels,
):
    cosine, sine = rotary_tables()
    crops = mesh_shape["crop"]
    seq = ("y", "z")

    swaps = []
    for crop in range(crops):
        for y in range(YS):
            slot = (y - crop % 2) % YS
            swaps.append((crop * YS + y, crop * YS + ((slot ^ 1) + crop % 2) % YS))

    send = pack(queries, keys, values, cosine, sine).reshape(SEQ, 3 * COLS, HEAD_DIM)
    mine = lax.all_to_all(send, seq, 0, 0, tiled=True)
    attended = attend(mine, lambda x: lax.ppermute(x, ("crop", "y"), swaps))
    returned = lax.all_to_all(attended, seq, 0, 0, tiled=True)

    strip_tokens = queries.shape[0]
    act = pl.pallas_call(
        features_kernel,
        in_specs=[VMEM] * 3,
        out_specs=VMEM,
        out_shape=jax.ShapeDtypeStruct((strip_tokens, CHANNELS), BF16),
        compiler_params=limit(12),
        name="features",
    )(returned, proj_weight, norm_gain.reshape(1, CHANNELS))
    far = lax.ppermute(act, seq, [(i, ((i + 1) ^ 1) - 1) for i in range(1, SEQ - 1)])
    pair = lax.ppermute(act, seq, [(i, i ^ 1) for i in range(SEQ)])
    rows, pixels = labels.shape
    logits, losses, sums = pl.pallas_call(
        head_kernel,
        in_specs=[VMEM] * 8,
        out_specs=[VMEM] * 3,
        out_shape=[
            pltpu.VMEM((CLASSES, rows, pixels), F32),
            pltpu.VMEM((rows, pixels), F32),
            pltpu.VMEM((SEQ, 1, HEAD_DIM), F32),
        ],
        scratch_shapes=[pltpu.VMEM((3 * strip_tokens, CHANNELS), BF16)],
        compiler_params=limit(12),
        name="head",
    )(
        pair, act, far, conv_weight, conv_bias.reshape(1, CHANNELS),
        class_weight.reshape(9 * CLASSES, CHANNELS), class_bias.reshape(CLASSES, 1), labels,
    )
    everyone = lax.all_to_all(sums, seq, 0, 0, tiled=True)
    loss = jnp.sum(everyone, axis=(0, 1))[:1]
    return logits, losses, loss


def solution(mesh):
    crops = mesh.shape["crop"]
    split = Mesh(mesh.devices.reshape(crops, YS, ZS), ("crop", "y", "z"))
    rows = P(("crop", "y", "z"), None)
    in_specs = (rows, rows, rows, P(), P(), P(), P(), P(), P(), rows)
    out_specs = (P(None, ("crop", "y", "z"), None), rows, P("crop"))
    return jax.shard_map(
        functools.partial(body, dict(split.shape)),
        mesh=split,
        in_specs=in_specs,
        out_specs=out_specs,
        check_vma=False,
    )
```

```python
import functools
import math

import jax
import jax.numpy as jnp
import numpy as np
from jax import lax
from jax.experimental import pallas as pl
from jax.experimental.pallas import tpu as pltpu
from jax.sharding import Mesh, PartitionSpec as P


HEADS = 16
HEAD_DIM = 128
UPSCALE = 4
COLS = 64
CHANNELS = 256
CLASSES = 16
YS = 4
ZS = 8
SEQ = YS * ZS
EPSILON = 1e-05
EXP_SCALE = HEAD_DIM**-0.5 * math.log2(math.e)
VMEM = pl.BlockSpec(memory_space=pltpu.VMEM)
BF16 = jnp.bfloat16
F32 = jnp.float32


def limit(mib):
    return pltpu.CompilerParams(vmem_limit_bytes=mib << 20)


def rotary_tables():
    quarter = HEAD_DIM // 4
    omegas = np.power(np.float32(100.0), -np.arange(quarter, dtype=np.float32) / np.float32(quarter))
    angles = np.arange(COLS, dtype=np.float32)[:, None] * omegas[None, :].astype(np.float32)
    cosine = np.cos(angles).astype(np.float32)
    sine = np.sin(angles).astype(np.float32)
    wide_cos = np.concatenate([cosine] * 4, axis=1)
    wide_sin = np.concatenate([-sine, sine, -sine, sine], axis=1)
    return wide_cos, wide_sin


def gelu(x):
    return x * (0.5 * (1.0 + lax.erf(x * np.float32(math.sqrt(0.5)))))


def positions():
    place = lax.axis_index("y") * ZS + lax.axis_index("z")
    return lax.rem(lax.axis_index("crop"), 2), place


HALVES = 2


def pack_kernel(q_hbm, k_hbm, v_hbm, cos_hbm, sin_hbm, out_ref, q_ref, k_ref, v_ref, cos_ref, sin_ref, sems, table_sems):
    core, place = positions()
    tables_in = [
        pltpu.make_async_copy(cos_hbm, cos_ref, table_sems.at[0]),
        pltpu.make_async_copy(sin_hbm, sin_ref, table_sems.at[1]),
    ]
    copies = []
    for half in range(HALVES):
        rows = pl.ds(half * COLS, COLS)
        copies.append(
            [
                pltpu.make_async_copy(hbm.at[rows], ref.at[rows], sems.at[half, which])
                for which, (hbm, ref) in enumerate(((q_hbm, q_ref), (k_hbm, k_ref), (v_hbm, v_ref)))
            ]
        )
        for copy in copies[-1]:
            copy.start()
        if half == 0:
            for copy in tables_in:
                copy.start()
    lane = lax.broadcasted_iota(jnp.int32, (COLS, HEAD_DIM), 1)
    by_row = lane < HEAD_DIM // 2
    first = (lane % (HEAD_DIM // 2)) < HEAD_DIM // 4
    for copy in tables_in:
        copy.wait()
    for half in range(HALVES):
        row = pl.ds(2 * place + half, 1)
        cosine, sine = [
            jnp.where(by_row, ref[row, :], ref[...]) for ref in (cos_ref, sin_ref)
        ]
        rows = slice(half * COLS, (half + 1) * COLS)
        for index, ref in ((0, q_ref), (1, k_ref), (2, v_ref)):
            copies[half][index].wait()
            for head in range(HEADS):
                y = lax.rem(2 * (head % 2) + half + core, YS)
                x = ref[rows, head * HEAD_DIM : (head + 1) * HEAD_DIM]
                if index < 2:
                    x = x.astype(F32)
                    partner = jnp.where(
                        first,
                        pltpu.roll(x, HEAD_DIM - HEAD_DIM // 4, 1),
                        pltpu.roll(x, HEAD_DIM // 4, 1),
                    )
                    x = (x * cosine + partner * sine).astype(BF16)
                out_ref[y, head // 2, index * COLS : (index + 1) * COLS, :] = x


def pack(queries, keys, values, cosine, sine):
    return pl.pallas_call(
        pack_kernel,
        in_specs=[pl.BlockSpec(memory_space=pltpu.HBM)] * 5,
        out_specs=VMEM,
        out_shape=jax.ShapeDtypeStruct((YS, ZS, 3 * COLS, HEAD_DIM), BF16),
        scratch_shapes=[pltpu.VMEM(queries.shape, BF16)] * 3
        + [pltpu.VMEM((COLS, HEAD_DIM), F32)] * 2
        + [pltpu.SemaphoreType.DMA((HALVES, 3)), pltpu.SemaphoreType.DMA((2,))],
        compiler_params=limit(8),
        name="pack",
    )(*(pltpu.with_memory_space_constraint(x, pltpu.HBM) for x in (queries, keys, values, cosine, sine)))


BLOCK = 4


def scores_of(query, key):
    return lax.dot_general(query, key, (((1,), (1,)), ((), ())), preferred_element_type=F32)


def with_ones(value):
    return jnp.concatenate([value, jnp.ones_like(value)], axis=1)


OWN_CHUNK = 512
MORE_CHUNK = 256
LAST_CHUNK = 768


def sweep(query, key, value, chunk):
    top = total = None
    for start in range(0, key.shape[0], chunk):
        scores = scores_of(query, key[start : start + chunk])
        before, top = top, jnp.max(scores, axis=1, keepdims=True)
        if before is not None:
            top = jnp.maximum(before, top)
        weights = jnp.exp2((scores - top) * EXP_SCALE).astype(BF16)
        part = jnp.dot(weights, value[start : start + chunk], preferred_element_type=F32)
        total = part if before is None else total * jnp.exp2((before - top) * EXP_SCALE) + part
    return jnp.broadcast_to(top, (query.shape[0], HEAD_DIM)), total


def keys_values(ref, first):
    tokens = ref.shape[0] * COLS
    key = ref[:, first : first + COLS, :].reshape(tokens, HEAD_DIM)
    value = ref[:, first + COLS : first + 2 * COLS, :].reshape(tokens, HEAD_DIM)
    return key, with_ones(value)


def each_block(visit):
    def step(i, carry):
        rows = BLOCK * COLS
        visit(pl.ds(i * BLOCK, BLOCK), pl.ds(pl.multiple_of(i * rows, rows), rows))
        return carry

    lax.fori_loop(0, SEQ // BLOCK, step, 0, unroll=SEQ // BLOCK)


def joined(one, two):
    top = jnp.maximum(one[0], two[0])
    fades = [jnp.exp2((side[0] - top) * EXP_SCALE) for side in (one, two)]
    mixed, norm = [
        one[1][:, lanes] * fades[0] + two[1][:, lanes] * fades[1]
        for lanes in (slice(0, HEAD_DIM), slice(HEAD_DIM, 2 * HEAD_DIM))
    ]
    return top, mixed, norm


def own_kernel(mine_ref, acc_ref, top_ref):
    key, value = keys_values(mine_ref, COLS)

    def visit(block, rows):
        query = mine_ref[block, :COLS, :].reshape(BLOCK * COLS, HEAD_DIM)
        top_ref[rows, :], acc_ref[rows, :] = sweep(query, key, value, OWN_CHUNK)

    each_block(visit)


def more_kernel(mine_ref, other_ref, acc_ref, top_ref, new_acc_ref, new_top_ref):
    key, value = keys_values(other_ref, 0)

    def visit(block, rows):
        query = mine_ref[block, :COLS, :].reshape(BLOCK * COLS, HEAD_DIM)
        top, mixed, norm = joined(sweep(query, key, value, MORE_CHUNK), (top_ref[rows, :], acc_ref[rows, :]))
        new_top_ref[rows, :] = top
        new_acc_ref[rows, :HEAD_DIM] = mixed
        new_acc_ref[rows, HEAD_DIM:] = norm

    each_block(visit)


def last_kernel(mine_ref, other_ref, acc_ref, top_ref, out_ref):
    key, value = keys_values(other_ref, 0)

    def visit(block, rows):
        query = mine_ref[block, :COLS, :].reshape(BLOCK * COLS, HEAD_DIM)
        _, mixed, norm = joined(sweep(query, key, value, LAST_CHUNK), (top_ref[rows, :], acc_ref[rows, :]))
        out_ref[block, :, :] = (mixed / norm).astype(BF16).reshape(BLOCK, COLS, HEAD_DIM)

    each_block(visit)


FIRST = 20


def attend(mine, swap):
    tokens = SEQ * COLS

    def cost(sources):
        pairs = tokens * sources * COLS
        return pl.CostEstimate(flops=6 * pairs * HEAD_DIM, bytes_accessed=4 << 20, transcendentals=pairs)

    running = [
        jax.ShapeDtypeStruct((tokens, 2 * HEAD_DIM), F32),
        jax.ShapeDtypeStruct((tokens, HEAD_DIM), F32),
    ]
    one = swap(mine[:FIRST, COLS:, :])
    two = swap(mine[FIRST:, COLS:, :])
    acc, top = pl.pallas_call(
        own_kernel,
        in_specs=[VMEM],
        out_specs=[VMEM, VMEM],
        out_shape=running,
        cost_estimate=cost(SEQ),
        compiler_params=limit(28),
        name="own_keys",
    )(mine)
    acc, top = pl.pallas_call(
        more_kernel,
        in_specs=[VMEM] * 4,
        out_specs=[VMEM, VMEM],
        out_shape=running,
        cost_estimate=cost(FIRST),
        compiler_params=limit(28),
        name="more_keys",
    )(mine, one, acc, top)
    return pl.pallas_call(
        last_kernel,
        in_specs=[VMEM] * 4,
        out_specs=VMEM,
        out_shape=jax.ShapeDtypeStruct((SEQ, COLS, HEAD_DIM), BF16),
        cost_estimate=cost(SEQ - FIRST),
        compiler_params=limit(28),
        name="last_keys",
    )(mine, two, acc, top)


def features_kernel(mixed_ref, proj_ref, gain_ref, out_ref):
    core, _ = positions()
    strips = []
    for half in range(2):
        pieces = []
        for head in range(HEADS):
            y = lax.rem(2 * (head % 2) + half + core, YS)
            pieces.append(mixed_ref[y * ZS + head // 2])
        strips.append(jnp.concatenate(pieces, axis=1))
    mixed = jnp.concatenate(strips, axis=0)
    features = jnp.dot(mixed, proj_ref[...], preferred_element_type=F32)
    center = jnp.mean(features, axis=-1, keepdims=True)
    spread = jnp.mean((features - center) ** 2, axis=-1, keepdims=True)
    normal = (features - center) / jnp.sqrt(spread + EPSILON) * gain_ref[...]
    out_ref[...] = gelu(normal).astype(BF16)


def head_kernel(
    pair_ref, mid_ref, far_ref, weight_ref, bias_ref, class_ref, class_bias_ref, labels_ref,
    logits_ref, losses_ref, sum_ref, act,
):
    _, place = positions()
    strip = 2
    odd = lax.rem(place, 2)
    edge = 2 * strip * COLS
    act[pl.ds(pl.multiple_of((1 - odd) * edge, strip * COLS), strip * COLS), :] = pair_ref[...]
    act[strip * COLS : edge, :] = mid_ref[...]
    act[pl.ds(pl.multiple_of(odd * edge, strip * COLS), strip * COLS), :] = far_ref[...]
    count = (strip + 2) * COLS
    stacked = jnp.concatenate([act[r * COLS : r * COLS + count] for r in range(3)], axis=1)
    products = []
    for s in range(3):
        weight = jnp.concatenate([weight_ref[3 * r + s] for r in range(3)], axis=0)
        products.append(jnp.dot(stacked, weight, preferred_element_type=F32))
    position = lax.broadcasted_iota(jnp.int32, (count, CHANNELS), 0)
    col = position % COLS
    total = products[1]
    total = total + jnp.where(col == 0, 0.0, pltpu.roll(products[0], 1, 0))
    total = total + jnp.where(col == COLS - 1, 0.0, pltpu.roll(products[2], count - 1, 0))
    hidden = gelu(total + bias_ref[...])
    grid_row = place * strip - 1 + position // COLS
    inside = (grid_row >= 0) & (grid_row < strip * SEQ)
    hidden = jnp.where(inside, hidden, 0.0).astype(BF16)

    taps = lax.dot_general(
        class_ref[...], hidden, (((1,), (1,)), ((), ())), preferred_element_type=F32
    )

    def tap(r, s, row):
        start = (3 * r + s) * CLASSES
        return taps[start : start + CLASSES, row * COLS : (row + 1) * COLS]

    sides = []
    for s in range(3):
        combos = []
        for row in (1, 2):
            t = [tap(r, s, row) for r in range(3)]
            combos.append(tap(0, s, row - 1) + t[1] + t[2])
            combos.append(t[0] + t[1] + t[2])
            combos.append(t[0] + t[1] + tap(2, s, row + 1))
        sides.append(jnp.concatenate(combos, axis=0))
    pixels = UPSCALE * COLS
    source = lax.broadcasted_iota(jnp.int32, (COLS, pixels), 0)
    target = lax.broadcasted_iota(jnp.int32, (COLS, pixels), 1)
    expands = []
    for s in range(3):
        first = UPSCALE * source - s + 1
        expands.append(
            jnp.where((target >= first) & (target < first + UPSCALE), 1.0, 0.0).astype(BF16)
        )
    side = jnp.concatenate(sides, axis=1)
    parts = []
    for _ in range(3):
        parts.append(side.astype(BF16))
        side = side - parts[-1].astype(F32)
    terms = jnp.dot(
        jnp.concatenate(parts, axis=0),
        jnp.concatenate(expands, axis=0),
        preferred_element_type=F32,
    )
    count = side.shape[0]
    spread_sum = terms[:count] + terms[count : 2 * count] + terms[2 * count :]
    class_ids = lax.broadcasted_iota(jnp.int32, (CLASSES, pixels), 0)
    loss_sum = jnp.zeros((1, pixels), F32)
    for combo in range(3 * strip):
        logits = spread_sum[combo * CLASSES : (combo + 1) * CLASSES] + class_bias_ref[...]
        highest = jnp.max(logits, axis=0, keepdims=True)
        log_total = highest + jnp.log(jnp.sum(jnp.exp(logits - highest), axis=0, keepdims=True))
        for inner in ((0,), (1, 2), (3,))[combo % 3]:
            y = UPSCALE * (combo // 3) + inner
            logits_ref[:, y, :] = logits
            chosen = class_ids == labels_ref[y : y + 1, :]
            picked = jnp.sum(jnp.where(chosen, logits, 0.0), axis=0, keepdims=True)
            loss = log_total - picked
            losses_ref[y : y + 1, :] = loss
            loss_sum = loss_sum + loss
    total_loss = jnp.sum(loss_sum, axis=1, keepdims=True) * (1.0 / (SEQ * losses_ref.size))
    sum_ref[...] = jnp.broadcast_to(total_loss[None], sum_ref.shape)


def body(
    mesh_shape, queries, keys, values, proj_weight, norm_gain, conv_weight, conv_bias, class_weight,
    class_bias, labels,
):
    cosine, sine = rotary_tables()
    crops = mesh_shape["crop"]
    seq = ("y", "z")

    swaps = []
    for crop in range(crops):
        for y in range(YS):
            slot = (y - crop % 2) % YS
            swaps.append((crop * YS + y, crop * YS + ((slot ^ 1) + crop % 2) % YS))

    send = pack(queries, keys, values, cosine, sine).reshape(SEQ, 3 * COLS, HEAD_DIM)
    mine = lax.all_to_all(send, seq, 0, 0, tiled=True)
    attended = attend(mine, lambda x: lax.ppermute(x, ("crop", "y"), swaps))
    returned = lax.all_to_all(attended, seq, 0, 0, tiled=True)

    strip_tokens = queries.shape[0]
    act = pl.pallas_call(
        features_kernel,
        in_specs=[VMEM] * 3,
        out_specs=VMEM,
        out_shape=jax.ShapeDtypeStruct((strip_tokens, CHANNELS), BF16),
        compiler_params=limit(12),
        name="features",
    )(returned, proj_weight, norm_gain.reshape(1, CHANNELS))
    far = lax.ppermute(act, seq, [(i, ((i + 1) ^ 1) - 1) for i in range(1, SEQ - 1)])
    pair = lax.ppermute(act, seq, [(i, i ^ 1) for i in range(SEQ)])
    rows, pixels = labels.shape
    logits, losses, sums = pl.pallas_call(
        head_kernel,
        in_specs=[VMEM] * 8,
        out_specs=[VMEM] * 3,
        out_shape=[
            jax.ShapeDtypeStruct((CLASSES, rows, pixels), F32),
            jax.ShapeDtypeStruct((rows, pixels), F32),
            jax.ShapeDtypeStruct((SEQ, 1, HEAD_DIM), F32),
        ],
        scratch_shapes=[pltpu.VMEM((3 * strip_tokens, CHANNELS), BF16)],
        compiler_params=limit(12),
        name="head",
    )(
        pair, act, far, conv_weight, conv_bias.reshape(1, CHANNELS),
        class_weight.reshape(9 * CLASSES, CHANNELS), class_bias.reshape(CLASSES, 1), labels,
    )
    everyone = lax.all_to_all(sums, seq, 0, 0, tiled=True)
    loss = jnp.sum(everyone, axis=(0, 1))[:1]
    return logits, losses, loss


def solution(mesh):
    crops = mesh.shape["crop"]
    split = Mesh(mesh.devices.reshape(crops, YS, ZS), ("crop", "y", "z"))
    rows = P(("crop", "y", "z"), None)
    in_specs = (rows, rows, rows, P(), P(), P(), P(), P(), P(), rows)
    out_specs = (P(None, ("crop", "y", "z"), None), rows, P("crop"))
    return jax.shard_map(
        functools.partial(body, dict(split.shape)),
        mesh=split,
        in_specs=in_specs,
        out_specs=out_specs,
        check_vma=False,
    )
```
